32 devices in a mesh: row: 8 (over y, x, core), col: 4 (over z).
Axes of the slice: x: 2, y: 2, z: 4, core: 2. Of those that a mesh axis runs over, the one named last changes fastest.
Arguments:
- normed: bfloat16 [96, 96, 128], P('row', 'col'), may hold values from -6 to 6
- left_proj: bfloat16 [128, 128], replicated, may hold values from -0.5 to 0.5
- left_gate: bfloat16 [128, 128], replicated, may hold values from -0.5 to 0.5
- right_proj: bfloat16 [128, 128], replicated, may hold values from -0.5 to 0.5
- right_gate: bfloat16 [128, 128], replicated, may hold values from -0.5 to 0.5
- out_gate: bfloat16 [128, 128], replicated, may hold values from -0.5 to 0.5
- out_proj: bfloat16 [128, 128], replicated, may hold values from -0.5 to 0.5
- hidden_norm_gain: float32 [128], replicated, may hold values from 0.1 to 1.9
- keep_bits: int32 [96, 8], P('col'), may hold values from 0 to 65535, as said below
- cotangent: bfloat16 [96, 96, 128], P('row', 'col'), may hold values from -6 to 6
Outputs:
- grad_normed: bfloat16 [96, 96, 128], P('row', 'col')
The draws below stay inside these ranges and needn't reach their ends.
Inputs may be any that keep to these rules, and one draw needn't show every extreme that they name: `keep_bits`: bit b (0 to 15) of entry [j, w] is the keep flag of channel 16 w + b in pair column j; the flags of a column hold for every row.
All inputs are finite; a program needn't handle non-finite values.
Results may differ from the reference program's by a relative error of at most 0.011.
Values may be sent and summed in bfloat16 or wider, within the bound.
A program may use at most 128 MiB of HBM per device.

```python
import jax
import jax.numpy as jnp
from jax import lax

C = 128
H = 128
N = 96


def draw_keep_bits(key, part):
    first_key = jax.random.fold_in(key, 11)
    second_key = jax.random.fold_in(key, 12)
    third_key = jax.random.fold_in(key, 13)
    first_words = jax.random.randint(first_key, (N, C // 16), 0, 65536, dtype=jnp.int32)
    second_words = jax.random.randint(second_key, (N, C // 16), 0, 65536, dtype=jnp.int32)
    packed_words = jnp.bitwise_or(first_words, second_words)
    chosen_row = jax.random.randint(third_key, (), 0, N, dtype=jnp.int32)
    packed_words = packed_words.at[chosen_row, 0].set(65535)
    return packed_words.astype(jnp.int32)


def level_of(rng, extent, pieces, smallest, largest):
    level = 1.0
    for position, blocks in pieces:
        steps = jax.random.uniform(jax.random.fold_in(jax.random.fold_in(rng, 6), position), (blocks,), jnp.float32, smallest / len(pieces), largest / len(pieces))
        level = level * jnp.repeat(jnp.exp(steps), extent[position] // blocks).reshape((-1,) + (1,) * (len(extent) - 1 - position))
    return level


def gaussian(own_key, shape, deviation, most, pieces=(), kind=jnp.bfloat16):
    values = jax.random.normal(own_key, shape, jnp.float32) * deviation
    if len(pieces) > 0:
        values = level_of(own_key, shape, pieces, -0.22, 0.18) * values
    return jnp.clip(values, min=-most, max=most).astype(kind)


def setup_inputs(seed: int = 0) -> dict:
    splits = jax.random.split(jax.random.key(seed), 11)
    normed = gaussian(splits[0], (N, N, C), 1.0, 6.0, ((0, 8), (1, 4)))
    left_proj = gaussian(splits[1], (C, H), C ** -0.5, 0.5)
    left_gate = gaussian(splits[2], (C, H), C ** -0.5, 0.5)
    right_proj = gaussian(splits[3], (C, H), C ** -0.5, 0.5)
    right_gate = gaussian(splits[4], (C, H), C ** -0.5, 0.5)
    out_gate = gaussian(splits[5], (C, C), C ** -0.5, 0.5)
    out_proj = gaussian(splits[6], (H, C), H ** -0.5, 0.5)
    hidden_norm_gain = jnp.clip(1.0 + 0.18 * jax.random.normal(splits[7], (H,), jnp.float32), 0.1, 1.9)
    keep_bits = draw_keep_bits(jax.random.fold_in(splits[10], 71), 0)
    cotangent = gaussian(splits[9], (N, N, C), 1.0, 6.0, ((0, 8), (1, 4)))
    return dict(normed=normed, left_proj=left_proj, left_gate=left_gate, right_proj=right_proj, right_gate=right_gate, out_gate=out_gate, out_proj=out_proj, hidden_norm_gain=hidden_norm_gain, keep_bits=keep_bits, cotangent=cotangent)


def unpack_keep(keep_bits):
    shifts = jnp.arange(16, dtype=jnp.int32)
    flags = jnp.bitwise_and(jnp.right_shift(keep_bits[:, :, None], shifts[None, None, :]), 1)
    return flags.reshape(keep_bits.shape[0], keep_bits.shape[1] * 16).astype(jnp.float32)

def gated_proj(block, weight_proj, weight_gate):
    linear = jnp.dot(block, weight_proj, preferred_element_type=jnp.float32)
    sigma = jax.nn.sigmoid(jnp.dot(block, weight_gate, preferred_element_type=jnp.float32))
    return (linear, sigma, (sigma * linear).astype(jnp.bfloat16))

def gate_back(grad, linear, sigma):
    return ((grad * sigma).astype(jnp.bfloat16), (grad * linear * sigma * (1.0 - sigma)).astype(jnp.bfloat16))

def reference(normed, left_proj, left_gate, right_proj, right_gate, out_gate, out_proj, hidden_norm_gain, keep_bits, cotangent):
    lin_a, sig_a, left = gated_proj(normed, left_proj, left_gate)
    lin_b, sig_b, right = gated_proj(normed, right_proj, right_gate)
    mixed = jnp.einsum('ikh,jkh->ijh', left.astype(jnp.float32), right.astype(jnp.float32), precision=lax.Precision.HIGHEST)
    average = lax.optimization_barrier(jnp.mean(mixed, axis=-1, keepdims=True))
    mean_removed = mixed - average
    inverse_deviation = lax.rsqrt(lax.optimization_barrier(jnp.mean(mean_removed * mean_removed, axis=-1, keepdims=True)) + 1e-05)
    standardized_input = mean_removed * inverse_deviation
    gain_vector = hidden_norm_gain.astype(jnp.float32)
    normalized_mixture = (standardized_input * gain_vector).astype(jnp.bfloat16)
    out_linear = jnp.dot(normalized_mixture, out_proj, preferred_element_type=jnp.float32)
    out_sigma = jax.nn.sigmoid(jnp.dot(normed, out_gate, preferred_element_type=jnp.float32))
    keep = unpack_keep(keep_bits)
    grad_out = cotangent.astype(jnp.float32) * keep[None, :, :] * (1.0 / 0.75)
    grad_linear, grad_gate_out = gate_back(grad_out, out_linear, out_sigma)
    norm_gradient = jnp.dot(grad_linear, out_proj.T, preferred_element_type=jnp.float32) * gain_vector
    mixed_gradient = inverse_deviation * (norm_gradient - lax.optimization_barrier(jnp.mean(norm_gradient, axis=-1, keepdims=True)) - standardized_input * lax.optimization_barrier(jnp.mean(norm_gradient * standardized_input, axis=-1, keepdims=True)))
    mixed_gradient = mixed_gradient.astype(jnp.bfloat16)
    grad_left = jnp.einsum('ijh,jkh->ikh', mixed_gradient.astype(jnp.float32), right.astype(jnp.float32), precision=lax.Precision.HIGHEST)
    grad_right = jnp.einsum('ijh,ikh->jkh', mixed_gradient.astype(jnp.float32), left.astype(jnp.float32), precision=lax.Precision.HIGHEST)
    grad_lin_a, grad_sig_a = gate_back(grad_left, lin_a, sig_a)
    grad_lin_b, grad_sig_b = gate_back(grad_right, lin_b, sig_b)
    stacked = jnp.concatenate([grad_lin_a, grad_sig_a, grad_lin_b, grad_sig_b, grad_gate_out], axis=-1)
    weights_t = jnp.concatenate([left_proj.T, left_gate.T, right_proj.T, right_gate.T, out_gate.T], axis=0)
    return jnp.dot(stacked, weights_t, preferred_element_type=jnp.float32).astype(jnp.bfloat16)
```

```python
import functools

import jax
import jax.numpy as jnp
from jax import lax
from jax.experimental import pallas as pl
from jax.experimental.pallas import tpu as pltpu
from jax.sharding import PartitionSpec as P

F32 = jnp.float32
BF16 = jnp.bfloat16
MESH = pl.DeviceIdType.MESH


def dot(a, b):
    return lax.dot_general(a, b, (((1,), (0,)), ((), ())), preferred_element_type=F32)


def dot_t(a, b):
    return lax.dot_general(a, b, (((1,), (1,)), ((), ())), preferred_element_type=F32)


def gate_back(grad, linear, sigma):
    part = grad * sigma
    return part.astype(BF16), (part * linear * (1.0 - sigma)).astype(BF16)


def mac(accs, steps, chunk, a_ref, a_row, b_ref, b_row, width):
    def some(block, accs):
        for u in range(chunk):
            t = block * chunk + u
            tile = b_ref[pl.ds(pl.multiple_of(b_row(t), 8), width), :]
            accs = tuple(
                acc + a_ref[pl.ds(a_row(i, t), 1), :] * tile for i, acc in enumerate(accs)
            )
        return accs

    return lax.fori_loop(0, steps // chunk, some, accs)


def kernel(
    rows,
    cols,
    ti,
    tj,
    x_ref,
    *refs,
):
    given, (out_ref, *held), scratch = refs[:9], refs[9:20], refs[20:]
    (lp_ref, lg_ref, rp_ref, rg_ref, og_ref, op_ref, gain_ref, keep_ref, cot_ref, own) = held
    (
        blocks,
        left,
        right,
        right_t,
        part_out,
        part_in,
        mixed,
        flat,
        split_a,
        split_b,
        panel,
        grad_in,
        wide,
        grad_l,
        lin_a,
        sig_a,
        lin_b,
        sig_b,
        grad_gate,
        a_send,
        f_send,
        a_recv,
        b_send,
        b_recv,
        c_send,
        c_recv,
        d_send,
        d_recv,
        load,
    ) = scratch
    r = lax.axis_index("row")
    c = lax.axis_index("col")
    chips = rows // 2
    q = lax.div(r, 2)
    core = lax.rem(r, 2)
    sibling = 2 * q + 1 - core
    cells = ti * tj
    half = ti * ti
    hidden = left.shape[1]

    def send(src, dst, send_sem, recv_sem, row, col):
        return pltpu.make_async_remote_copy(
            src_ref=src,
            dst_ref=dst,
            send_sem=send_sem,
            recv_sem=recv_sem,
            device_id=(row, col),
            device_id_type=MESH,
        )

    def chip_at(d):
        high = lax.rem(lax.div(q, 2) + lax.rem(d, chips // 2), chips // 2)
        return 2 * high + lax.rem(lax.rem(q, 2) + lax.div(d, chips // 2), 2)

    def row_at(d):
        return lax.rem(r + d, rows)

    def col_at(d):
        return lax.rem(c + d, cols)

    def first(d, src_row):
        to = 2 * chip_at(d) + core
        return send(x_ref, blocks.at[src_row], a_send.at[d], a_recv.at[src_row], to, c)

    def to_sibling(src, src_row, sem):
        return send(src, blocks.at[src_row], sem, a_recv.at[src_row], sibling, c)

    def near(n):
        least = jnp.minimum(c, cols - 1 - c)
        both = (lax.div(n, 2) + 1) * (1 - 2 * lax.rem(n, 2))
        longer = (n - least + 1) * jnp.where(2 * c < cols, 1, -1)
        return c + jnp.where(n < 2 * least, both, longer)

    def part(h, to, slot):
        return send(
            part_out.at[h, to], part_in.at[h, slot], b_send.at[h, to], b_recv.at[h, slot], r, to
        )

    def across(h, to, slot):
        return send(
            panel.at[c, h], panel.at[slot, h], c_send.at[h, to], c_recv.at[h, slot], r, to
        )

    def onward(src_col, h, slot):
        to = 2 * src_col + h
        return send(
            panel.at[src_col, h], grad_in.at[slot], d_send.at[to], d_recv.at[slot], to, c
        )

    barrier = pltpu.get_barrier_semaphore()

    def greet_row(d, _):
        pl.semaphore_signal(barrier, inc=1, device_id=(row_at(d), c), device_id_type=MESH)
        return 0

    def greet_col(d, _):
        pl.semaphore_signal(barrier, inc=1, device_id=(r, col_at(d)), device_id_type=MESH)
        return 0

    lax.fori_loop(1, rows, greet_row, 0)
    lax.fori_loop(1, cols, greet_col, 0)
    loads = [
        pltpu.make_async_copy(src, dst, load.at[n])
        for n, (src, dst) in enumerate(zip((*given, x_ref), held))
    ]
    for one in loads:
        one.start()
    for one in loads:
        one.wait()

    def spread(flat_value, dst):
        flat[...] = flat_value
        for h in range(2):
            for i in range(ti):
                dst[h, i * ti : (i + 1) * ti, :] = flat[
                    i * tj + h * ti : i * tj + (h + 1) * ti, :
                ]

    words = keep_ref[...]
    depth = words.shape[0]
    lane = lax.broadcasted_iota(jnp.int32, (depth, hidden), 1)
    pick = (lane // 16 == lax.broadcasted_iota(jnp.int32, (depth, hidden), 0)).astype(BF16)

    def by_lane(value):
        return lax.dot_general(
            value.astype(F32).astype(BF16),
            pick,
            (((0,), (0,)), ((), ())),
            preferred_element_type=F32,
        ).astype(jnp.int32)

    low = by_lane(jnp.bitwise_and(words, 255))
    high = by_lane(jnp.right_shift(words, 8))
    bit = lax.broadcasted_iota(jnp.int32, (tj, hidden), 1) % 16
    keep = jnp.bitwise_and(jnp.right_shift(low + high * 256, bit), 1).astype(F32)
    spread(
        (cot_ref[...].astype(F32).reshape(ti, tj, hidden) * keep[None]).reshape(cells, hidden)
        * (1.0 / 0.75),
        split_a,
    )

    w_left = jnp.concatenate([lp_ref[...], lg_ref[...]], axis=1)
    w_right = jnp.concatenate([rp_ref[...], rg_ref[...]], axis=1)

    def gated(x, weights):
        both = dot(x, weights)
        return both[:, :hidden], jax.nn.sigmoid(both[:, hidden:])

    pad = right_t.shape[0] // tj

    def keep_right(value, row):
        right[pl.ds(pl.multiple_of(row * cells, 8), cells), :] = value
        for j in range(ti):
            right_t[pl.ds(j, tj, stride=pad), :] = value[j * tj : (j + 1) * tj]

    def project(x, row):
        base = pl.multiple_of(row * cells, 8)
        linear, sigma = gated(x, w_left)
        left[pl.ds(base, cells), :] = (sigma * linear).astype(BF16).astype(F32)
        linear, sigma = gated(x, w_right)
        keep_right((sigma * linear).astype(BF16).astype(F32), row)

    def zeros(count, width):
        return tuple(jnp.zeros((width, hidden), F32) for _ in range(count))

    def share(chip, h):
        accs = mac(
            zeros(ti, pad),
            tj,
            2,
            left,
            lambda i, t: r * cells + i * tj + t,
            right_t,
            lambda t: t * pad,
            pad,
        )
        for i, acc in enumerate(accs):
            wide[i * ti : (i + 1) * ti, :] = acc[:ti]

        @pl.when(chip == c)
        def _():
            mixed[h] = wide[:half, :]

        @pl.when(chip != c)
        def _():
            part_out[h, chip] = wide[:half, :].astype(BF16)

    def share_send(chip, h):
        @pl.when(chip != c)
        def _():
            part(h, chip, c).start()

    x = own[...]
    linear, sigma = gated(x, w_left)
    lin_a[...] = linear
    sig_a[...] = sigma
    left[pl.ds(pl.multiple_of(r * cells, 8), cells), :] = (sigma * linear).astype(BF16).astype(F32)
    linear, sigma = gated(x, w_right)
    lin_b[...] = linear
    sig_b[...] = sigma
    keep_right((sigma * linear).astype(BF16).astype(F32), r)
    share(q, core)
    spread(jax.nn.sigmoid(dot(x, og_ref[...])), split_b)
    gain = gain_ref[...]

    pl.semaphore_wait(barrier, rows - 1 + cols - 1)

    def start_first(d, _):
        first(d, r).start()
        return 0

    lax.fori_loop(1, chips, start_first, 0)
    to_sibling(x_ref, r, a_send.at[0]).start()

    share_send(q, core)

    def relay(d, _):
        row = 2 * chip_at(d) + core
        first(d, row).wait_recv()
        to_sibling(blocks.at[row], row, f_send.at[d]).start()
        return 0

    def direct(d, _):
        chip = chip_at(d)
        row = 2 * chip + core
        project(blocks[row], row)
        share(chip, core)
        share_send(chip, core)
        return 0

    def relayed(d, _):
        chip = chip_at(d)
        row = 2 * chip + 1 - core
        to_sibling(x_ref, row, a_send.at[0]).wait_recv()
        project(blocks[row], row)
        share(chip, 1 - core)
        share_send(chip, 1 - core)
        return 0

    relayed(0, 0)
    lax.fori_loop(1, chips - 1, relay, 0)
    lax.fori_loop(1, chips - 1, direct, 0)
    lax.fori_loop(1, chips - 1, relayed, 0)
    relay(chips - 1, 0)
    direct(chips - 1, 0)
    relayed(chips - 1, 0)

    def norm_half(s, _):
        h = lax.rem(core + s, 2)

        def take_part(n, total):
            slot = near(n)
            part(h, slot, slot).wait_recv()
            return total + part_in[h, slot].astype(F32)

        value = lax.fori_loop(0, cols - 1, take_part, mixed[h])
        out_sigma = split_b[h]
        removed = value - jnp.mean(value, axis=-1, keepdims=True)
        inverse = lax.rsqrt(jnp.mean(removed * removed, axis=-1, keepdims=True) + 1e-05)
        standard = removed * inverse
        out_linear = dot((standard * gain).astype(BF16), op_ref[...])
        grad_part = split_a[h] * out_sigma
        norm = dot_t(grad_part.astype(BF16), op_ref[...]) * gain
        panel[c, h] = (
            inverse
            * (
                norm
                - jnp.mean(norm, axis=-1, keepdims=True)
                - standard * jnp.mean(norm * standard, axis=-1, keepdims=True)
            )
        ).astype(BF16)
        split_a[h] = grad_part * out_linear * (1.0 - out_sigma)

        def start_across(n, _):
            across(h, near(cols - 2 - n), c).start()
            return 0

        lax.fori_loop(0, cols - 1, start_across, 0)
        return 0

    lax.fori_loop(0, 2, norm_half, 0)
    for h in range(2):
        for i in range(ti):
            flat[i * tj + h * ti : i * tj + (h + 1) * ti, :] = split_a[
                h, i * ti : (i + 1) * ti, :
            ]
    grad_gate[...] = flat[...].astype(BF16)
    grad_l[...] = jnp.zeros((cells, hidden), F32)

    def panel_at(n):
        step = lax.rem(n, cols)
        h = lax.rem(core + lax.div(n, cols), 2)
        return step, h, jnp.where(step == 0, c, near(step - 1))

    def forward(n, _):
        step, h, col = panel_at(n)

        @pl.when(step > 0)
        def _():
            across(h, col, col).wait_recv()

        to = 2 * col + h

        @pl.when(to != r)
        def _():
            onward(col, h, r).start()

        @pl.when(to == r)
        def _():
            grad_in[r] = panel[col, h]

        return 0

    def take_half(n, _):
        step, h, col = panel_at(n)
        to = 2 * col + h
        wide[:half, :] = panel[col, h].astype(F32)
        accs = mac(
            tuple(grad_l[i * tj : (i + 1) * tj, :] for i in range(ti)),
            ti,
            2,
            wide,
            lambda i, t: i * ti + t,
            right,
            lambda t: to * cells + t * tj,
            tj,
        )
        for i, acc in enumerate(accs):
            grad_l[i * tj : (i + 1) * tj, :] = acc
        return 0

    def forward_take(n, _):
        forward(n, 0)
        return take_half(n, 0)

    def take_grad(d, accs):
        row = 2 * chip_at(lax.rem(d, chips)) + lax.rem(core + lax.div(d, chips), 2)

        @pl.when(d > 0)
        def _():
            onward(c, 0, row).wait_recv()

        wide[:half, :] = grad_in[row].astype(F32)
        return mac(
            accs,
            ti,
            2,
            wide,
            lambda i, t: t * ti + i,
            left,
            lambda t: row * cells + t * tj,
            tj,
        )

    lax.fori_loop(0, 2 * cols - 1, forward_take, 0)
    forward_take(2 * cols - 1, 0)
    accs = lax.fori_loop(0, chips, take_grad, zeros(ti, tj))
    for i, acc in enumerate(accs):
        flat[i * tj : (i + 1) * tj, :] = acc
    accs = tuple(flat[i * tj : (i + 1) * tj, :] for i in range(ti))
    accs = lax.fori_loop(chips, rows, take_grad, accs)
    for i, acc in enumerate(accs):
        flat[i * tj : (i + 1) * tj, :] = acc

    from_left = jnp.concatenate(gate_back(grad_l[...], lin_a[...], sig_a[...]), axis=1)
    from_right = jnp.concatenate(gate_back(flat[...], lin_b[...], sig_b[...]), axis=1)
    out_ref[...] = (
        dot_t(from_left, w_left) + dot_t(from_right, w_right) + dot_t(grad_gate[...], og_ref[...])
    ).astype(BF16)

    def end_chip(d, _):
        first(d, r).wait_send()
        to_sibling(x_ref, r, f_send.at[d]).wait_send()
        return 0

    lax.fori_loop(1, chips, end_chip, 0)
    to_sibling(x_ref, r, a_send.at[0]).wait_send()

    def end_col(d, _):
        col = col_at(d)
        for h in range(2):
            part(h, col, c).wait_send()
            across(h, col, c).wait_send()
        return 0

    lax.fori_loop(1, cols, end_col, 0)

    def end_row(d, _):
        to = row_at(d)
        send(
            panel.at[c, 0], grad_in.at[r], d_send.at[to], d_recv.at[r], to, c
        ).wait_send()
        return 0

    lax.fori_loop(1, rows, end_row, 0)


def body(rows, cols, normed, lp, lg, rp, rg, og, op, gain, keep_bits, cotangent):
    ti, tj, width = normed.shape
    hidden = lp.shape[1]
    assert tj == 2 * ti and rows == 2 * cols
    cells = ti * tj
    half = ti * ti
    tile = pltpu.VMEM((cells, hidden), F32)
    dma = pltpu.SemaphoreType.DMA
    out = pl.pallas_call(
        functools.partial(kernel, rows, cols, ti, tj),
        out_shape=pltpu.VMEM((cells, width), BF16),
        in_specs=[pl.BlockSpec(memory_space=pl.ANY)] * 10,
        out_specs=pl.BlockSpec(memory_space=pltpu.VMEM),
        scratch_shapes=[
            *[pltpu.VMEM((width, hidden), BF16)] * 6,
            pltpu.VMEM((1, hidden), F32),
            pltpu.VMEM(keep_bits.shape[::-1], jnp.int32),
            pltpu.VMEM((cells, width), BF16),
            pltpu.VMEM((cells, width), BF16),
            pltpu.VMEM((rows, cells, width), BF16),
            pltpu.VMEM((rows * cells, hidden), F32),
            pltpu.VMEM((rows * cells, hidden), F32),
            pltpu.VMEM((tj * (-(-ti // 8) * 8), hidden), F32),
            pltpu.VMEM((2, cols, half, hidden), BF16),
            pltpu.VMEM((2, cols, half, hidden), BF16),
            pltpu.VMEM((2, half, hidden), F32),
            tile,
            pltpu.VMEM((2, half, hidden), F32),
            pltpu.VMEM((2, half, hidden), F32),
            pltpu.VMEM((cols, 2, half, hidden), BF16),
            pltpu.VMEM((rows, half, hidden), BF16),
            tile,
            tile,
            tile,
            tile,
            tile,
            tile,
            pltpu.VMEM((cells, width), BF16),
            dma((rows // 2,)),
            dma((rows // 2,)),
            dma((rows,)),
            dma((2, cols)),
            dma((2, cols)),
            dma((2, cols)),
            dma((2, cols)),
            dma((rows,)),
            dma((rows,)),
            dma((10,)),
        ],
        compiler_params=pltpu.CompilerParams(
            collective_id=0, has_side_effects=True, vmem_limit_bytes=56 * 1024 * 1024
        ),
    )(
        normed.reshape(cells, width),
        lp,
        lg,
        rp,
        rg,
        og,
        op,
        gain.reshape(1, hidden),
        keep_bits.T,
        cotangent.reshape(cells, width),
    )
    return out.reshape(ti, tj, width)


def solution(mesh):
    whole = P("row", "col", None)
    return jax.shard_map(
        functools.partial(body, mesh.shape["row"], mesh.shape["col"]),
        mesh=mesh,
        in_specs=(whole, P(), P(), P(), P(), P(), P(), P(), P("col", None), whole),
        out_specs=whole,
        check_vma=False,
    )
```

```python
import functools

import jax
import jax.numpy as jnp
from jax import lax
from jax.experimental import pallas as pl
from jax.experimental.pallas import tpu as pltpu
from jax.sharding import PartitionSpec as P

F32 = jnp.float32
BF16 = jnp.bfloat16
MESH = pl.DeviceIdType.MESH


def dot(a, b):
    return lax.dot_general(a, b, (((1,), (0,)), ((), ())), preferred_element_type=F32)


def dot_t(a, b):
    return lax.dot_general(a, b, (((1,), (1,)), ((), ())), preferred_element_type=F32)


def gate_back(grad, linear, sigma):
    part = grad * sigma
    return part.astype(BF16), (part * linear * (1.0 - sigma)).astype(BF16)


def mac(accs, steps, chunk, a_ref, a_row, b_ref, b_row, width):
    def some(block, accs):
        for u in range(chunk):
            t = block * chunk + u
            tile = b_ref[pl.ds(pl.multiple_of(b_row(t), 8), width), :]
            accs = tuple(
                acc + a_ref[pl.ds(a_row(i, t), 1), :] * tile for i, acc in enumerate(accs)
            )
        return accs

    return lax.fori_loop(0, steps // chunk, some, accs)


def kernel(
    rows,
    cols,
    ti,
    tj,
    x_ref,
    *refs,
):
    given, (out_ref, *held), scratch = refs[:9], refs[9:20], refs[20:]
    (lp_ref, lg_ref, rp_ref, rg_ref, og_ref, op_ref, gain_ref, keep_ref, cot_ref, own) = held
    (
        blocks,
        left,
        right,
        right_t,
        part_out,
        part_in,
        mixed,
        flat,
        split_a,
        split_b,
        panel,
        grad_in,
        wide,
        grad_l,
        lin_a,
        sig_a,
        lin_b,
        sig_b,
        grad_gate,
        a_send,
        f_send,
        a_recv,
        b_send,
        b_recv,
        c_send,
        c_recv,
        d_send,
        d_recv,
        load,
        grad_r,
        total,
        grad_lin,
        mixed_x,
        part_in_x,
        grad_x,
        norm_x,
        norm_back,
        x_recv,
        g_send,
        g_recv,
        xc_send,
        n_send,
        n_recv,
    ) = scratch
    r = lax.axis_index("row")
    c = lax.axis_index("col")
    chips = rows // 2
    q = lax.div(r, 2)
    core = lax.rem(r, 2)
    sibling = 2 * q + 1 - core
    cells = ti * tj
    half = ti * ti
    hidden = left.shape[1]

    def send(src, dst, send_sem, recv_sem, row, col):
        return pltpu.make_async_remote_copy(
            src_ref=src,
            dst_ref=dst,
            send_sem=send_sem,
            recv_sem=recv_sem,
            device_id=(row, col),
            device_id_type=MESH,
        )

    def chip_at(d):
        high = lax.rem(lax.div(q, 2) + lax.rem(d, chips // 2), chips // 2)
        return 2 * high + lax.rem(lax.rem(q, 2) + lax.div(d, chips // 2), 2)

    def row_at(d):
        return lax.rem(r + d, rows)

    def col_at(d):
        return lax.rem(c + d, cols)

    def first(d, src_row):
        to = 2 * chip_at(d) + core
        return send(x_ref, blocks.at[src_row], a_send.at[d], a_recv.at[src_row], to, c)

    def to_sibling(src, src_row, sem):
        return send(src, blocks.at[src_row], sem, a_recv.at[src_row], sibling, c)

    def near(n):
        least = jnp.minimum(c, cols - 1 - c)
        both = (lax.div(n, 2) + 1) * (1 - 2 * lax.rem(n, 2))
        longer = (n - least + 1) * jnp.where(2 * c < cols, 1, -1)
        return c + jnp.where(n < 2 * least, both, longer)

    def part(h, to, slot):
        return send(
            part_out.at[h, to], part_in.at[h, slot], b_send.at[h, to], b_recv.at[h, slot], r, to
        )

    def across(h, to, slot):
        return send(
            panel.at[c, h], panel.at[slot, h], c_send.at[h, to], c_recv.at[h, slot], r, to
        )

    def middle(h):
        return cols // 2 - 1 + h

    def part_x(h, slot):
        return send(
            part_out.at[h, last],
            part_in_x.at[slot],
            b_send.at[h, last],
            x_recv.at[slot],
            r,
            middle(h),
        )

    def across_x(to, h, col):
        return send(
            panel.at[col, h], panel.at[col, h], xc_send.at[to], c_recv.at[h, col], r, to
        )

    def lend(h):
        return send(grad_lin.at[h], grad_x, g_send.at[h], g_recv, r, middle(h))

    def give_back(h):
        return send(norm_x, norm_back.at[h], n_send, n_recv.at[h], r, last)

    def onward(src_col, h, slot):
        to = 2 * src_col + h
        return send(
            panel.at[src_col, h], grad_in.at[slot], d_send.at[to], d_recv.at[slot], to, c
        )

    last = chip_at(chips - 1)
    side = c - middle(0)
    central = (side >= 0) & (side < 2)
    barrier = pltpu.get_barrier_semaphore()

    def greet_row(d, _):
        pl.semaphore_signal(barrier, inc=1, device_id=(row_at(d), c), device_id_type=MESH)
        return 0

    def greet_col(d, _):
        pl.semaphore_signal(barrier, inc=1, device_id=(r, col_at(d)), device_id_type=MESH)
        return 0

    lax.fori_loop(1, rows, greet_row, 0)
    lax.fori_loop(1, cols, greet_col, 0)
    loads = [
        pltpu.make_async_copy(src, dst, load.at[n])
        for n, (src, dst) in enumerate(zip((*given, x_ref), held))
    ]
    for one in loads:
        one.start()
    for one in loads:
        one.wait()

    def spread(flat_value, dst):
        flat[...] = flat_value
        for h in range(2):
            for i in range(ti):
                dst[h, i * ti : (i + 1) * ti, :] = flat[
                    i * tj + h * ti : i * tj + (h + 1) * ti, :
                ]

    words = keep_ref[...]
    depth = words.shape[0]
    lane = lax.broadcasted_iota(jnp.int32, (depth, hidden), 1)
    pick = (lane // 16 == lax.broadcasted_iota(jnp.int32, (depth, hidden), 0)).astype(BF16)

    def by_lane(value):
        return lax.dot_general(
            value.astype(F32).astype(BF16),
            pick,
            (((0,), (0,)), ((), ())),
            preferred_element_type=F32,
        ).astype(jnp.int32)

    low = by_lane(jnp.bitwise_and(words, 255))
    high = by_lane(jnp.right_shift(words, 8))
    bit = lax.broadcasted_iota(jnp.int32, (tj, hidden), 1) % 16
    keep = jnp.bitwise_and(jnp.right_shift(low + high * 256, bit), 1).astype(F32)
    spread(
        (cot_ref[...].astype(F32).reshape(ti, tj, hidden) * keep[None]).reshape(cells, hidden)
        * (1.0 / 0.75),
        split_a,
    )

    w_left = jnp.concatenate([lp_ref[...], lg_ref[...]], axis=1)
    w_right = jnp.concatenate([rp_ref[...], rg_ref[...]], axis=1)

    def gated(x, weights):
        both = dot(x, weights)
        return both[:, :hidden], jax.nn.sigmoid(both[:, hidden:])

    pad = right_t.shape[0] // tj

    def keep_right(value, row):
        right[pl.ds(pl.multiple_of(row * cells, 8), cells), :] = value
        for j in range(ti):
            right_t[pl.ds(j, tj, stride=pad), :] = value[j * tj : (j + 1) * tj]

    def project(x, row):
        base = pl.multiple_of(row * cells, 8)
        linear, sigma = gated(x, w_left)
        left[pl.ds(base, cells), :] = (sigma * linear).astype(BF16).astype(F32)
        linear, sigma = gated(x, w_right)
        keep_right((sigma * linear).astype(BF16).astype(F32), row)

    def zeros(count, width):
        return tuple(jnp.zeros((width, hidden), F32) for _ in range(count))

    def share(chip, h, final=False):
        accs = mac(
            zeros(ti, pad),
            tj,
            2,
            left,
            lambda i, t: r * cells + i * tj + t,
            right_t,
            lambda t: t * pad,
            pad,
        )
        for i, acc in enumerate(accs):
            wide[i * ti : (i + 1) * ti, :] = acc[:ti]

        here = middle(h) if final else chip

        @pl.when(here == c)
        def _():
            if final:
                mixed_x[...] = wide[:half, :]
            else:
                mixed[h] = wide[:half, :]

        @pl.when(here != c)
        def _():
            part_out[h, chip] = wide[:half, :].astype(BF16)

    def share_send(chip, h, final=False):
        here = middle(h) if final else chip

        @pl.when(here != c)
        def _():
            if final:
                part_x(h, c).start()
            else:
                part(h, chip, c).start()

    x = own[...]
    linear, sigma = gated(x, w_left)
    lin_a[...] = linear
    sig_a[...] = sigma
    left[pl.ds(pl.multiple_of(r * cells, 8), cells), :] = (sigma * linear).astype(BF16).astype(F32)
    linear, sigma = gated(x, w_right)
    lin_b[...] = linear
    sig_b[...] = sigma
    keep_right((sigma * linear).astype(BF16).astype(F32), r)
    share(q, core)
    spread(jax.nn.sigmoid(dot(x, og_ref[...])), split_b)
    gain = gain_ref[...]

    pl.semaphore_wait(barrier, rows - 1 + cols - 1)

    def start_first(d, _):
        first(d, r).start()
        return 0

    lax.fori_loop(1, chips, start_first, 0)
    to_sibling(x_ref, r, a_send.at[0]).start()

    share_send(q, core)

    @pl.when(c == last)
    def _():
        for h in range(2):
            split_a[h] = split_a[h] * split_b[h]
            grad_lin[h] = split_a[h].astype(BF16)

            @pl.when(middle(h) == c)
            def _():
                grad_x[...] = grad_lin[h]

            @pl.when(middle(h) != c)
            def _():
                lend(h).start()

    def relay(d, _):
        row = 2 * chip_at(d) + core
        first(d, row).wait_recv()
        to_sibling(blocks.at[row], row, f_send.at[d]).start()
        return 0

    def direct(d, _, final=False):
        chip = chip_at(d)
        row = 2 * chip + core
        project(blocks[row], row)
        share(chip, core, final)
        share_send(chip, core, final)
        return 0

    def relayed(d, _, final=False):
        chip = chip_at(d)
        row = 2 * chip + 1 - core
        to_sibling(x_ref, row, a_send.at[0]).wait_recv()
        project(blocks[row], row)
        share(chip, 1 - core, final)
        share_send(chip, 1 - core, final)
        return 0

    relayed(0, 0)
    lax.fori_loop(1, chips - 1, relay, 0)
    lax.fori_loop(1, chips - 1, direct, 0)
    lax.fori_loop(1, chips - 1, relayed, 0)
    relay(chips - 1, 0)
    direct(chips - 1, 0, True)
    relayed(chips - 1, 0, True)

    def norm_both(value, grad_part):
        removed = value - jnp.mean(value, axis=-1, keepdims=True)
        inverse = lax.rsqrt(jnp.mean(removed * removed, axis=-1, keepdims=True) + 1e-05)
        standard = removed * inverse
        norm = dot_t(grad_part, op_ref[...]) * gain
        back = inverse * (
            norm
            - jnp.mean(norm, axis=-1, keepdims=True)
            - standard * jnp.mean(norm * standard, axis=-1, keepdims=True)
        )
        return (standard * gain).astype(BF16), back.astype(BF16)

    def norm_half(s, _):
        h = lax.rem(core + s, 2)

        def take_part(n, total):
            slot = near(n)
            part(h, slot, slot).wait_recv()
            return total + part_in[h, slot].astype(F32)

        value = lax.fori_loop(0, cols - 1, take_part, mixed[h])
        out_sigma = split_b[h]
        grad_part = split_a[h] * out_sigma
        normed_mix, panel[c, h] = norm_both(value, grad_part.astype(BF16))

        def start_across(n, _):
            across(h, near(cols - 2 - n), c).start()
            return 0

        lax.fori_loop(0, cols - 1, start_across, 0)
        out_linear = dot(normed_mix, op_ref[...])
        split_a[h] = grad_part * out_linear * (1.0 - out_sigma)
        return 0

    @pl.when(c != last)
    def _():
        lax.fori_loop(0, 2, norm_half, 0)

    @pl.when(central)
    def _():
        @pl.when(c != last)
        def _():
            lend(side).wait_recv()

        def take_part(n, total):
            slot = near(n)
            part_x(side, slot).wait_recv()
            return total + part_in_x[slot].astype(F32)

        value = lax.fori_loop(0, cols - 1, take_part, mixed_x[...])
        normed_mix, panel[last, side] = norm_both(value, grad_x[...])

        def start_across(n, _):
            across_x(near(cols - 2 - n), side, last).start()
            return 0

        lax.fori_loop(0, cols - 1, start_across, 0)

        @pl.when(c == last)
        def _():
            norm_back[side] = normed_mix

        @pl.when(c != last)
        def _():
            norm_x[...] = normed_mix
            give_back(side).start()

    grad_l[...] = jnp.zeros((cells, hidden), F32)

    def seen(n, total):
        return total + jnp.where(near(n) == last, n + 1, 0)

    place = lax.fori_loop(0, cols - 1, seen, 0)

    def panel_at(n):
        step = lax.div(n, 2)
        turn = jnp.where(step < place, step, step + 1)
        near_by = jnp.where(turn == 0, c, near(turn - 1))
        col = jnp.where(step == cols - 1, last, near_by)
        return step, lax.rem(core + lax.rem(n, 2), 2), col

    def forward(n, _):
        step, h, col = panel_at(n)

        maker = jnp.where(col == last, middle(h), col)

        @pl.when(maker != c)
        def _():
            across(h, col, col).wait_recv()

        to = 2 * col + h

        @pl.when(to != r)
        def _():
            onward(col, h, r).start()

        @pl.when(to == r)
        def _():
            grad_in[r] = panel[col, h]

        return 0

    def take_half(n, _):
        step, h, col = panel_at(n)
        to = 2 * col + h
        wide[:half, :] = panel[col, h].astype(F32)
        accs = mac(
            tuple(grad_l[i * tj : (i + 1) * tj, :] for i in range(ti)),
            ti,
            2,
            wide,
            lambda i, t: i * ti + t,
            right,
            lambda t: to * cells + t * tj,
            tj,
        )
        for i, acc in enumerate(accs):
            grad_l[i * tj : (i + 1) * tj, :] = acc
        return 0

    def forward_take(n, _):
        forward(n, 0)
        return take_half(n, 0)

    def take_grad(d, accs):
        row = 2 * chip_at(lax.div(d, 2)) + lax.rem(core + lax.rem(d, 2), 2)

        @pl.when(d > 0)
        def _():
            onward(c, 0, row).wait_recv()

        wide[:half, :] = grad_in[row].astype(F32)
        return mac(
            accs,
            ti,
            2,
            wide,
            lambda i, t: t * ti + i,
            left,
            lambda t: row * cells + t * tj,
            tj,
        )

    def from_gate():
        @pl.when(c == last)
        def _():
            for h in range(2):

                @pl.when(middle(h) != c)
                def _():
                    give_back(h).wait_recv()

                out_linear = dot(norm_back[h], op_ref[...])
                split_a[h] = split_a[h] * out_linear * (1.0 - split_b[h])

        for h in range(2):
            for i in range(ti):
                flat[i * tj + h * ti : i * tj + (h + 1) * ti, :] = split_a[
                    h, i * ti : (i + 1) * ti, :
                ]
        grad_gate[...] = flat[...].astype(BF16)
        total[...] = dot_t(grad_gate[...], og_ref[...])

    def some_grads(first_row, last_row):
        accs = tuple(grad_r[i * tj : (i + 1) * tj, :] for i in range(ti))
        accs = lax.fori_loop(first_row, last_row, take_grad, accs)
        for i, acc in enumerate(accs):
            grad_r[i * tj : (i + 1) * tj, :] = acc

    def from_left():
        back = gate_back(grad_l[...], lin_a[...], sig_a[...])
        return dot_t(jnp.concatenate(back, axis=1), w_left)

    def from_right():
        back = gate_back(grad_r[...], lin_b[...], sig_b[...])
        return dot_t(jnp.concatenate(back, axis=1), w_right)

    lax.fori_loop(0, 2 * cols - 2, forward_take, 0)

    soon = 2 * chips - 2
    grad_r[...] = jnp.zeros((cells, hidden), F32)

    @pl.when(c == q)
    def _():
        from_gate()
        some_grads(0, soon)

    lax.fori_loop(2 * cols - 2, 2 * cols, forward_take, 0)

    @pl.when(c != q)
    def _():
        from_gate()
        total[...] += from_left()
        some_grads(0, rows)
        out_ref[...] = (total[...] + from_right()).astype(BF16)

    @pl.when(c == q)
    def _():
        total[...] += from_left()
        some_grads(soon, rows)
        out_ref[...] = (total[...] + from_right()).astype(BF16)

    def end_chip(d, _):
        first(d, r).wait_send()
        to_sibling(x_ref, r, f_send.at[d]).wait_send()
        return 0

    lax.fori_loop(1, chips, end_chip, 0)
    to_sibling(x_ref, r, a_send.at[0]).wait_send()

    def end_col(d, _):
        col = col_at(d)
        for h in range(2):

            @pl.when(col != last)
            def _():
                part(h, col, c).wait_send()

            @pl.when(c != last)
            def _():
                across(h, col, c).wait_send()

        @pl.when(central)
        def _():
            across_x(col, side, last).wait_send()

        return 0

    for h in range(2):

        @pl.when(middle(h) != c)
        def _():
            part_x(h, c).wait_send()

            @pl.when(c == last)
            def _():
                lend(h).wait_send()

    @pl.when(central & (c != last))
    def _():
        give_back(side).wait_send()

    lax.fori_loop(1, cols, end_col, 0)

    def end_row(d, _):
        to = row_at(d)
        send(
            panel.at[c, 0], grad_in.at[r], d_send.at[to], d_recv.at[r], to, c
        ).wait_send()
        return 0

    lax.fori_loop(1, rows, end_row, 0)


def body(rows, cols, normed, lp, lg, rp, rg, og, op, gain, keep_bits, cotangent):
    ti, tj, width = normed.shape
    hidden = lp.shape[1]
    assert tj == 2 * ti and rows == 2 * cols
    cells = ti * tj
    half = ti * ti
    tile = pltpu.VMEM((cells, hidden), F32)
    dma = pltpu.SemaphoreType.DMA
    out = pl.pallas_call(
        functools.partial(kernel, rows, cols, ti, tj),
        out_shape=pltpu.VMEM((cells, width), BF16),
        in_specs=[pl.BlockSpec(memory_space=pl.ANY)] * 10,
        out_specs=pl.BlockSpec(memory_space=pltpu.VMEM),
        scratch_shapes=[
            *[pltpu.VMEM((width, hidden), BF16)] * 6,
            pltpu.VMEM((1, hidden), F32),
            pltpu.VMEM(keep_bits.shape[::-1], jnp.int32),
            pltpu.VMEM((cells, width), BF16),
            pltpu.VMEM((cells, width), BF16),
            pltpu.VMEM((rows, cells, width), BF16),
            pltpu.VMEM((rows * cells, hidden), F32),
            pltpu.VMEM((rows * cells, hidden), F32),
            pltpu.VMEM((tj * (-(-ti // 8) * 8), hidden), F32),
            pltpu.VMEM((2, cols, half, hidden), BF16),
            pltpu.VMEM((2, cols, half, hidden), BF16),
            pltpu.VMEM((2, half, hidden), F32),
            tile,
            pltpu.VMEM((2, half, hidden), F32),
            pltpu.VMEM((2, half, hidden), F32),
            pltpu.VMEM((cols, 2, half, hidden), BF16),
            pltpu.VMEM((rows, half, hidden), BF16),
            tile,
            tile,
            tile,
            tile,
            tile,
            tile,
            pltpu.VMEM((cells, width), BF16),
            dma((rows // 2,)),
            dma((rows // 2,)),
            dma((rows,)),
            dma((2, cols)),
            dma((2, cols)),
            dma((2, cols)),
            dma((2, cols)),
            dma((rows,)),
            dma((rows,)),
            dma((10,)),
            tile,
            tile,
            pltpu.VMEM((2, half, hidden), BF16),
            pltpu.VMEM((half, hidden), F32),
            pltpu.VMEM((cols, half, hidden), BF16),
            pltpu.VMEM((half, hidden), BF16),
            pltpu.VMEM((half, hidden), BF16),
            pltpu.VMEM((2, half, hidden), BF16),
            dma((cols,)),
            dma((2,)),
            dma,
            dma((cols,)),
            dma,
            dma((2,)),
        ],
        compiler_params=pltpu.CompilerParams(
            collective_id=0, has_side_effects=True, vmem_limit_bytes=56 * 1024 * 1024
        ),
    )(
        normed.reshape(cells, width),
        lp,
        lg,
        rp,
        rg,
        og,
        op,
        gain.reshape(1, hidden),
        keep_bits.T,
        cotangent.reshape(cells, width),
    )
    return out.reshape(ti, tj, width)


def solution(mesh):
    whole = P("row", "col", None)
    return jax.shard_map(
        functools.partial(body, mesh.shape["row"], mesh.shape["col"]),
        mesh=mesh,
        in_specs=(whole, P(), P(), P(), P(), P(), P(), P(), P("col", None), whole),
        out_specs=whole,
        check_vma=False,
    )
```

```python
import functools

import jax
import jax.numpy as jnp
from jax import lax
from jax.experimental import pallas as pl
from jax.experimental.pallas import tpu as pltpu
from jax.sharding import PartitionSpec as P

F32 = jnp.float32
BF16 = jnp.bfloat16
MESH = pl.DeviceIdType.MESH


def dot(a, b):
    return lax.dot_general(a, b, (((1,), (0,)), ((), ())), preferred_element_type=F32)


def dot_t(a, b):
    return lax.dot_general(a, b, (((1,), (1,)), ((), ())), preferred_element_type=F32)


def gate_back(grad, linear, sigma):
    part = grad * sigma
    return part.astype(BF16), (part * linear * (1.0 - sigma)).astype(BF16)


def mac(accs, steps, chunk, a_ref, a_row, b_ref, b_row, width):
    def some(block, accs):
        for u in range(chunk):
            t = block * chunk + u
            tile = b_ref[pl.ds(pl.multiple_of(b_row(t), 8), width), :]
            accs = tuple(
                acc + a_ref[pl.ds(a_row(i, t), 1), :] * tile for i, acc in enumerate(accs)
            )
        return accs

    return lax.fori_loop(0, steps // chunk, some, accs)


def kernel(
    rows,
    cols,
    ti,
    tj,
    x_ref,
    *refs,
):
    given, (out_ref, *held), scratch = refs[:9], refs[9:20], refs[20:]
    (lp_ref, lg_ref, rp_ref, rg_ref, og_ref, op_ref, gain_ref, keep_ref, cot_ref, own) = held
    (
        blocks,
        left,
        right,
        right_t,
        part_out,
        part_in,
        mixed,
        flat,
        split_a,
        split_b,
        panel,
        grad_in,
        wide,
        grad_l,
        lin_a,
        sig_a,
        lin_b,
        sig_b,
        grad_gate,
        a_send,
        f_send,
        a_recv,
        b_send,
        b_recv,
        c_send,
        c_recv,
        d_send,
        d_recv,
        load,
        grad_r,
        total,
        grad_lin,
        mixed_x,
        part_in_x,
        grad_x,
        norm_x,
        norm_back,
        x_recv,
        g_send,
        g_recv,
        xc_send,
        n_send,
        n_recv,
        p_send,
    ) = scratch
    r = lax.axis_index("row")
    c = lax.axis_index("col")
    chips = rows // 2
    q = lax.div(r, 2)
    core = lax.rem(r, 2)
    sibling = 2 * q + 1 - core
    cells = ti * tj
    half = ti * ti
    hidden = left.shape[1]

    def send(src, dst, send_sem, recv_sem, row, col):
        return pltpu.make_async_remote_copy(
            src_ref=src,
            dst_ref=dst,
            send_sem=send_sem,
            recv_sem=recv_sem,
            device_id=(row, col),
            device_id_type=MESH,
        )

    def chip_at(d):
        high = lax.rem(lax.div(q, 2) + lax.rem(d, chips // 2), chips // 2)
        return 2 * high + lax.rem(lax.rem(q, 2) + lax.div(d, chips // 2), 2)

    def row_at(d):
        return lax.rem(r + d, rows)

    def col_at(d):
        return lax.rem(c + d, cols)

    def first(d, src_row):
        to = 2 * chip_at(d) + core
        return send(x_ref, blocks.at[src_row], a_send.at[d], a_recv.at[src_row], to, c)

    def to_sibling(src, src_row, sem):
        return send(src, blocks.at[src_row], sem, a_recv.at[src_row], sibling, c)

    def near(n):
        least = jnp.minimum(c, cols - 1 - c)
        both = (lax.div(n, 2) + 1) * (1 - 2 * lax.rem(n, 2))
        longer = (n - least + 1) * jnp.where(2 * c < cols, 1, -1)
        return c + jnp.where(n < 2 * least, both, longer)

    def part(h, to, slot):
        return send(
            part_out.at[h, to], part_in.at[h, slot], b_send.at[h, to], b_recv.at[h, slot], r, to
        )

    def across(h, to, slot):
        return send(
            panel.at[c, h], panel.at[slot, h], c_send.at[h, to], c_recv.at[h, slot], r, to
        )

    def gate(src):
        return jnp.where(2 * src < cols, cols // 2, cols // 2 - 1)

    def beyond(src, to):
        return ((2 * src < cols) != (2 * to < cols)) & (to != gate(src))

    def passed(h, to):
        return send(
            panel.at[q, h], panel.at[q, h], p_send.at[h, to], c_recv.at[h, q], r, to
        )

    def middle(h):
        return cols // 2 - 1 + h

    def part_x(h, slot):
        return send(
            part_out.at[h, last],
            part_in_x.at[slot],
            b_send.at[h, last],
            x_recv.at[slot],
            r,
            middle(h),
        )

    def across_x(to, h, col):
        return send(
            panel.at[col, h], panel.at[col, h], xc_send.at[to], c_recv.at[h, col], r, to
        )

    def lend(h):
        return send(grad_lin.at[h], grad_x, g_send.at[h], g_recv, r, middle(h))

    def give_back(h):
        return send(norm_x, norm_back.at[h], n_send, n_recv.at[h], r, last)

    def onward(src_col, h, slot):
        to = 2 * src_col + h
        return send(
            panel.at[src_col, h], grad_in.at[slot], d_send.at[to], d_recv.at[slot], to, c
        )

    last = chip_at(chips - 1)
    side = c - middle(0)
    central = (side >= 0) & (side < 2)
    barrier = pltpu.get_barrier_semaphore()

    def greet_row(d, _):
        pl.semaphore_signal(barrier, inc=1, device_id=(row_at(d), c), device_id_type=MESH)
        return 0

    def greet_col(d, _):
        pl.semaphore_signal(barrier, inc=1, device_id=(r, col_at(d)), device_id_type=MESH)
        return 0

    lax.fori_loop(1, rows, greet_row, 0)
    lax.fori_loop(1, cols, greet_col, 0)
    loads = [
        pltpu.make_async_copy(src, dst, load.at[n])
        for n, (src, dst) in enumerate(zip((*given, x_ref), held))
    ]
    for one in loads:
        one.start()
    for one in loads:
        one.wait()

    def spread(flat_value, dst):
        flat[...] = flat_value
        for h in range(2):
            for i in range(ti):
                dst[h, i * ti : (i + 1) * ti, :] = flat[
                    i * tj + h * ti : i * tj + (h + 1) * ti, :
                ]

    words = keep_ref[...]
    depth = words.shape[0]
    lane = lax.broadcasted_iota(jnp.int32, (depth, hidden), 1)
    pick = (lane // 16 == lax.broadcasted_iota(jnp.int32, (depth, hidden), 0)).astype(BF16)

    def by_lane(value):
        return lax.dot_general(
            value.astype(F32).astype(BF16),
            pick,
            (((0,), (0,)), ((), ())),
            preferred_element_type=F32,
        ).astype(jnp.int32)

    low = by_lane(jnp.bitwise_and(words, 255))
    high = by_lane(jnp.right_shift(words, 8))
    bit = lax.broadcasted_iota(jnp.int32, (tj, hidden), 1) % 16
    keep = jnp.bitwise_and(jnp.right_shift(low + high * 256, bit), 1).astype(F32)
    spread(
        (cot_ref[...].astype(F32).reshape(ti, tj, hidden) * keep[None]).reshape(cells, hidden)
        * (1.0 / 0.75),
        split_a,
    )

    w_left = jnp.concatenate([lp_ref[...], lg_ref[...]], axis=1)
    w_right = jnp.concatenate([rp_ref[...], rg_ref[...]], axis=1)

    def gated(x, weights):
        both = dot(x, weights)
        return both[:, :hidden], jax.nn.sigmoid(both[:, hidden:])

    pad = right_t.shape[0] // tj

    def keep_right(value, row):
        right[pl.ds(pl.multiple_of(row * cells, 8), cells), :] = value
        for j in range(ti):
            right_t[pl.ds(j, tj, stride=pad), :] = value[j * tj : (j + 1) * tj]

    def project_left(row):
        linear, sigma = gated(blocks[row], w_left)
        base = pl.multiple_of(row * cells, 8)
        left[pl.ds(base, cells), :] = (sigma * linear).astype(BF16).astype(F32)

    def other_left(d, _):
        project_left(row_at(d))
        return 0

    def project(x, row):
        linear, sigma = gated(x, w_right)
        keep_right((sigma * linear).astype(BF16).astype(F32), row)

    def zeros(count, width):
        return tuple(jnp.zeros((width, hidden), F32) for _ in range(count))

    def share(chip, h, final=False):
        accs = mac(
            zeros(ti, pad),
            tj,
            2,
            left,
            lambda i, t: r * cells + i * tj + t,
            right_t,
            lambda t: t * pad,
            pad,
        )
        for i, acc in enumerate(accs):
            wide[i * ti : (i + 1) * ti, :] = acc[:ti]

        here = middle(h) if final else chip

        @pl.when(here == c)
        def _():
            if final:
                mixed_x[...] = wide[:half, :]
            else:
                mixed[h] = wide[:half, :]

        @pl.when(here != c)
        def _():
            part_out[h, chip] = wide[:half, :].astype(BF16)

    def share_send(chip, h, final=False):
        here = middle(h) if final else chip

        @pl.when(here != c)
        def _():
            if final:
                part_x(h, c).start()
            else:
                part(h, chip, c).start()

    x = own[...]
    linear, sigma = gated(x, w_left)
    lin_a[...] = linear
    sig_a[...] = sigma
    left[pl.ds(pl.multiple_of(r * cells, 8), cells), :] = (sigma * linear).astype(BF16).astype(F32)
    linear, sigma = gated(x, w_right)
    lin_b[...] = linear
    sig_b[...] = sigma
    keep_right((sigma * linear).astype(BF16).astype(F32), r)
    share(q, core)
    spread(jax.nn.sigmoid(dot(x, og_ref[...])), split_b)
    gain = gain_ref[...]

    pl.semaphore_wait(barrier, rows - 1 + cols - 1)

    def start_first(d, _):
        first(d, r).start()
        return 0

    lax.fori_loop(1, chips, start_first, 0)
    to_sibling(x_ref, r, a_send.at[0]).start()

    share_send(q, core)

    @pl.when(c == last)
    def _():
        for h in range(2):
            split_a[h] = split_a[h] * split_b[h]
            grad_lin[h] = split_a[h].astype(BF16)

            @pl.when(middle(h) == c)
            def _():
                grad_x[...] = grad_lin[h]

            @pl.when(middle(h) != c)
            def _():
                lend(h).start()

    def relay(d, _):
        row = 2 * chip_at(d) + core
        first(d, row).wait_recv()
        to_sibling(blocks.at[row], row, f_send.at[d]).start()
        return 0

    def direct(d, _, final=False):
        chip = chip_at(d)
        row = 2 * chip + core
        project(blocks[row], row)
        share(chip, core, final)
        share_send(chip, core, final)
        return 0

    def relayed(d, _, final=False):
        chip = chip_at(d)
        row = 2 * chip + 1 - core
        to_sibling(x_ref, row, a_send.at[0]).wait_recv()
        project(blocks[row], row)
        share(chip, 1 - core, final)
        share_send(chip, 1 - core, final)
        return 0

    relayed(0, 0)
    lax.fori_loop(1, chips - 1, relay, 0)
    lax.fori_loop(1, chips - 1, direct, 0)
    lax.fori_loop(1, chips - 1, relayed, 0)
    relay(chips - 1, 0)
    direct(chips - 1, 0, True)
    relayed(chips - 1, 0, True)

    def norm_both(value, grad_part):
        removed = value - jnp.mean(value, axis=-1, keepdims=True)
        inverse = lax.rsqrt(jnp.mean(removed * removed, axis=-1, keepdims=True) + 1e-05)
        standard = removed * inverse
        norm = dot_t(grad_part, op_ref[...]) * gain
        back = inverse * (
            norm
            - jnp.mean(norm, axis=-1, keepdims=True)
            - standard * jnp.mean(norm * standard, axis=-1, keepdims=True)
        )
        return (standard * gain).astype(BF16), back.astype(BF16)

    def norm_half(s, _):
        h = lax.rem(core + s, 2)

        def take_part(n, total):
            slot = near(n)
            part(h, slot, slot).wait_recv()
            return total + part_in[h, slot].astype(F32)

        value = lax.fori_loop(0, cols - 1, take_part, mixed[h])
        out_sigma = split_b[h]
        grad_part = split_a[h] * out_sigma
        normed_mix, panel[c, h] = norm_both(value, grad_part.astype(BF16))

        def start_across(n, _):
            to = near(cols - 2 - n)

            @pl.when((c != q) | jnp.logical_not(beyond(c, to)))
            def _():
                across(h, to, c).start()

            return 0

        lax.fori_loop(0, cols - 1, start_across, 0)
        out_linear = dot(normed_mix, op_ref[...])
        split_a[h] = grad_part * out_linear * (1.0 - out_sigma)
        return 0

    @pl.when(core == 1)
    def _():
        lax.fori_loop(1, rows, other_left, 0)

    @pl.when(c != last)
    def _():
        lax.fori_loop(0, 2, norm_half, 0)

    @pl.when(central)
    def _():
        @pl.when(c != last)
        def _():
            lend(side).wait_recv()

        def take_part(n, total):
            slot = near(n)
            part_x(side, slot).wait_recv()
            return total + part_in_x[slot].astype(F32)

        value = lax.fori_loop(0, cols - 1, take_part, mixed_x[...])
        normed_mix, panel[last, side] = norm_both(value, grad_x[...])

        def start_across(n, _):
            across_x(near(cols - 2 - n), side, last).start()
            return 0

        lax.fori_loop(0, cols - 1, start_across, 0)

        @pl.when(c == last)
        def _():
            norm_back[side] = normed_mix

        @pl.when(c != last)
        def _():
            norm_x[...] = normed_mix
            give_back(side).start()

    @pl.when(c == gate(q))
    def _():
        for s in range(2):
            h = lax.rem(core + s, 2)
            across(h, q, q).wait_recv()

            def pass_on(n, _):
                to = col_at(n)

                @pl.when(beyond(q, to))
                def _():
                    passed(h, to).start()

                return 0

            lax.fori_loop(1, cols, pass_on, 0)

    @pl.when(core == 0)
    def _():
        lax.fori_loop(1, rows, other_left, 0)

    grad_l[...] = jnp.zeros((cells, hidden), F32)

    far = beyond(q, c)

    def place_of(col):
        def seen(n, total):
            return total + jnp.where(near(n) == col, n + 1, 0)

        return lax.fori_loop(0, cols - 1, seen, 0)

    last_place = place_of(last)
    own_place = jnp.where(far, place_of(q), cols)
    low = jnp.minimum(last_place, own_place)
    high = jnp.maximum(last_place, own_place)

    def panel_at(n):
        step = lax.div(n, 2)
        turn = step + jnp.where(step >= low, 1, 0)
        turn = turn + jnp.where(turn >= high, 1, 0)
        col = jnp.where(turn == 0, c, near(turn - 1))
        at_last = jnp.where(far, cols - 2, cols - 1)
        col = jnp.where(step == at_last, last, jnp.where(step > at_last, q, col))
        return step, lax.rem(core + lax.rem(n, 2), 2), col

    def forward(n, _):
        step, h, col = panel_at(n)

        maker = jnp.where(col == last, middle(h), col)

        @pl.when((maker != c) & ((col != q) | (c != gate(q))))
        def _():
            across(h, col, col).wait_recv()

        to = 2 * col + h

        @pl.when(to != r)
        def _():
            onward(col, h, r).start()

        @pl.when(to == r)
        def _():
            grad_in[r] = panel[col, h]

        return 0

    def take_half(n, _):
        step, h, col = panel_at(n)
        to = 2 * col + h
        wide[:half, :] = panel[col, h].astype(F32)
        accs = mac(
            tuple(grad_l[i * tj : (i + 1) * tj, :] for i in range(ti)),
            ti,
            2,
            wide,
            lambda i, t: i * ti + t,
            right,
            lambda t: to * cells + t * tj,
            tj,
        )
        for i, acc in enumerate(accs):
            grad_l[i * tj : (i + 1) * tj, :] = acc
        return 0

    def forward_take(n, _):
        forward(n, 0)
        return take_half(n, 0)

    def take_grad(d, accs):
        row = 2 * chip_at(lax.div(d, 2)) + lax.rem(core + lax.rem(d, 2), 2)

        @pl.when(d > 0)
        def _():
            onward(c, 0, row).wait_recv()

        wide[:half, :] = grad_in[row].astype(F32)
        return mac(
            accs,
            ti,
            2,
            wide,
            lambda i, t: t * ti + i,
            left,
            lambda t: row * cells + t * tj,
            tj,
        )

    def from_gate():
        @pl.when(c == last)
        def _():
            for h in range(2):

                @pl.when(middle(h) != c)
                def _():
                    give_back(h).wait_recv()

                out_linear = dot(norm_back[h], op_ref[...])
                split_a[h] = split_a[h] * out_linear * (1.0 - split_b[h])

        for h in range(2):
            for i in range(ti):
                flat[i * tj + h * ti : i * tj + (h + 1) * ti, :] = split_a[
                    h, i * ti : (i + 1) * ti, :
                ]
        grad_gate[...] = flat[...].astype(BF16)
        total[...] = dot_t(grad_gate[...], og_ref[...])

    def some_grads(first_row, last_row):
        accs = tuple(grad_r[i * tj : (i + 1) * tj, :] for i in range(ti))
        accs = lax.fori_loop(first_row, last_row, take_grad, accs)
        for i, acc in enumerate(accs):
            grad_r[i * tj : (i + 1) * tj, :] = acc

    def from_left():
        back = gate_back(grad_l[...], lin_a[...], sig_a[...])
        return dot_t(jnp.concatenate(back, axis=1), w_left)

    def from_right():
        back = gate_back(grad_r[...], lin_b[...], sig_b[...])
        return dot_t(jnp.concatenate(back, axis=1), w_right)

    lax.fori_loop(0, 2 * cols - 2, forward_take, 0)

    soon = 2 * chips - 2
    grad_r[...] = jnp.zeros((cells, hidden), F32)

    @pl.when(c == q)
    def _():
        from_gate()
        some_grads(0, soon)

    lax.fori_loop(2 * cols - 2, 2 * cols, forward_take, 0)

    @pl.when(c != q)
    def _():
        from_gate()
        total[...] += from_left()
        some_grads(0, rows)
        out_ref[...] = (total[...] + from_right()).astype(BF16)

    @pl.when(c == q)
    def _():
        total[...] += from_left()
        some_grads(soon, rows)
        out_ref[...] = (total[...] + from_right()).astype(BF16)

    def end_chip(d, _):
        first(d, r).wait_send()
        to_sibling(x_ref, r, f_send.at[d]).wait_send()
        return 0

    lax.fori_loop(1, chips, end_chip, 0)
    to_sibling(x_ref, r, a_send.at[0]).wait_send()

    def end_col(d, _):
        col = col_at(d)
        for h in range(2):

            @pl.when(col != last)
            def _():
                part(h, col, c).wait_send()

            @pl.when((c != last) & ((c != q) | jnp.logical_not(beyond(c, col))))
            def _():
                across(h, col, c).wait_send()

            @pl.when((c == gate(q)) & beyond(q, col))
            def _():
                passed(h, col).wait_send()

        @pl.when(central)
        def _():
            across_x(col, side, last).wait_send()

        return 0

    for h in range(2):

        @pl.when(middle(h) != c)
        def _():
            part_x(h, c).wait_send()

            @pl.when(c == last)
            def _():
                lend(h).wait_send()

    @pl.when(central & (c != last))
    def _():
        give_back(side).wait_send()

    lax.fori_loop(1, cols, end_col, 0)

    def end_row(d, _):
        to = row_at(d)
        send(
            panel.at[c, 0], grad_in.at[r], d_send.at[to], d_recv.at[r], to, c
        ).wait_send()
        return 0

    lax.fori_loop(1, rows, end_row, 0)


def body(rows, cols, normed, lp, lg, rp, rg, og, op, gain, keep_bits, cotangent):
    ti, tj, width = normed.shape
    hidden = lp.shape[1]
    assert tj == 2 * ti and rows == 2 * cols
    cells = ti * tj
    half = ti * ti
    tile = pltpu.VMEM((cells, hidden), F32)
    dma = pltpu.SemaphoreType.DMA
    out = pl.pallas_call(
        functools.partial(kernel, rows, cols, ti, tj),
        out_shape=pltpu.VMEM((cells, width), BF16),
        in_specs=[pl.BlockSpec(memory_space=pl.ANY)] * 10,
        out_specs=pl.BlockSpec(memory_space=pltpu.VMEM),
        scratch_shapes=[
            *[pltpu.VMEM((width, hidden), BF16)] * 6,
            pltpu.VMEM((1, hidden), F32),
            pltpu.VMEM(keep_bits.shape[::-1], jnp.int32),
            pltpu.VMEM((cells, width), BF16),
            pltpu.VMEM((cells, width), BF16),
            pltpu.VMEM((rows, cells, width), BF16),
            pltpu.VMEM((rows * cells, hidden), F32),
            pltpu.VMEM((rows * cells, hidden), F32),
            pltpu.VMEM((tj * (-(-ti // 8) * 8), hidden), F32),
            pltpu.VMEM((2, cols, half, hidden), BF16),
            pltpu.VMEM((2, cols, half, hidden), BF16),
            pltpu.VMEM((2, half, hidden), F32),
            tile,
            pltpu.VMEM((2, half, hidden), F32),
            pltpu.VMEM((2, half, hidden), F32),
            pltpu.VMEM((cols, 2, half, hidden), BF16),
            pltpu.VMEM((rows, half, hidden), BF16),
            tile,
            tile,
            tile,
            tile,
            tile,
            tile,
            pltpu.VMEM((cells, width), BF16),
            dma((rows // 2,)),
            dma((rows // 2,)),
            dma((rows,)),
            dma((2, cols)),
            dma((2, cols)),
            dma((2, cols)),
            dma((2, cols)),
            dma((rows,)),
            dma((rows,)),
            dma((10,)),
            tile,
            tile,
            pltpu.VMEM((2, half, hidden), BF16),
            pltpu.VMEM((half, hidden), F32),
            pltpu.VMEM((cols, half, hidden), BF16),
            pltpu.VMEM((half, hidden), BF16),
            pltpu.VMEM((half, hidden), BF16),
            pltpu.VMEM((2, half, hidden), BF16),
            dma((cols,)),
            dma((2,)),
            dma,
            dma((cols,)),
            dma,
            dma((2,)),
            dma((2, cols)),
        ],
        compiler_params=pltpu.CompilerParams(
            collective_id=0, has_side_effects=True, vmem_limit_bytes=56 * 1024 * 1024
        ),
    )(
        normed.reshape(cells, width),
        lp,
        lg,
        rp,
        rg,
        og,
        op,
        gain.reshape(1, hidden),
        keep_bits.T,
        cotangent.reshape(cells, width),
    )
    return out.reshape(ti, tj, width)


def solution(mesh):
    whole = P("row", "col", None)
    return jax.shard_map(
        functools.partial(body, mesh.shape["row"], mesh.shape["col"]),
        mesh=mesh,
        in_specs=(whole, P(), P(), P(), P(), P(), P(), P(), P("col", None), whole),
        out_specs=whole,
        check_vma=False,
    )
```

```python
import functools

import jax
import jax.numpy as jnp
from jax import lax
from jax.experimental import pallas as pl
from jax.experimental.pallas import tpu as pltpu
from jax.sharding import PartitionSpec as P

F32 = jnp.float32
BF16 = jnp.bfloat16
MESH = pl.DeviceIdType.MESH


def dot(a, b):
    return lax.dot_general(a, b, (((1,), (0,)), ((), ())), preferred_element_type=F32)


def dot_t(a, b):
    return lax.dot_general(a, b, (((1,), (1,)), ((), ())), preferred_element_type=F32)


def gate_back(grad, linear, sigma):
    part = grad * sigma
    return part.astype(BF16), (part * linear * (1.0 - sigma)).astype(BF16)


def mac(accs, steps, chunk, a_ref, a_row, b_ref, b_row, width):
    def some(block, accs):
        for u in range(chunk):
            t = block * chunk + u
            tile = b_ref[pl.ds(pl.multiple_of(b_row(t), 8), width), :]
            accs = tuple(
                acc + a_ref[pl.ds(a_row(i, t), 1), :] * tile for i, acc in enumerate(accs)
            )
        return accs

    return lax.fori_loop(0, steps // chunk, some, accs)


def kernel(
    rows,
    cols,
    ti,
    tj,
    x_ref,
    *refs,
):
    given, (out_ref, *held), scratch = refs[:9], refs[9:20], refs[20:]
    (lp_ref, lg_ref, rp_ref, rg_ref, og_ref, op_ref, gain_ref, keep_ref, cot_ref, own) = held
    (
        blocks,
        left,
        right,
        right_t,
        part_out,
        part_in,
        mixed,
        flat,
        split_a,
        split_b,
        panel,
        grad_in,
        wide,
        grad_l,
        lin_a,
        sig_a,
        lin_b,
        sig_b,
        grad_gate,
        a_send,
        f_send,
        a_recv,
        b_send,
        b_recv,
        c_send,
        c_recv,
        d_send,
        d_recv,
        load,
        grad_r,
        total,
        grad_lin,
        mixed_x,
        part_in_x,
        grad_x,
        norm_x,
        norm_back,
        x_recv,
        g_send,
        g_recv,
        xc_send,
        n_send,
        n_recv,
        p_send,
        s_send,
    ) = scratch
    r = lax.axis_index("row")
    c = lax.axis_index("col")
    chips = rows // 2
    q = lax.div(r, 2)
    core = lax.rem(r, 2)
    sibling = 2 * q + 1 - core
    cells = ti * tj
    half = ti * ti
    hidden = left.shape[1]

    def send(src, dst, send_sem, recv_sem, row, col):
        return pltpu.make_async_remote_copy(
            src_ref=src,
            dst_ref=dst,
            send_sem=send_sem,
            recv_sem=recv_sem,
            device_id=(row, col),
            device_id_type=MESH,
        )

    def chip_at(d):
        high = lax.rem(lax.div(q, 2) + lax.rem(d, chips // 2), chips // 2)
        return 2 * high + lax.rem(lax.rem(q, 2) + lax.div(d, chips // 2), 2)

    def row_at(d):
        return lax.rem(r + d, rows)

    def col_at(d):
        return lax.rem(c + d, cols)

    def first(d, src_row):
        to = 2 * chip_at(d) + core
        return send(x_ref, blocks.at[src_row], a_send.at[d], a_recv.at[src_row], to, c)

    def to_sibling(src, src_row, sem):
        return send(src, blocks.at[src_row], sem, a_recv.at[src_row], sibling, c)

    def near(n):
        least = jnp.minimum(c, cols - 1 - c)
        both = (lax.div(n, 2) + 1) * (1 - 2 * lax.rem(n, 2))
        longer = (n - least + 1) * jnp.where(2 * c < cols, 1, -1)
        return c + jnp.where(n < 2 * least, both, longer)

    def part(h, to, slot):
        return send(
            part_out.at[h, to], part_in.at[h, slot], b_send.at[h, to], b_recv.at[h, slot], r, to
        )

    def across(h, to, slot):
        return send(
            panel.at[c, h], panel.at[slot, h], c_send.at[h, to], c_recv.at[h, slot], r, to
        )

    def gate(src):
        return jnp.where(2 * src < cols, cols // 2, cols // 2 - 1)

    def beyond(src, to):
        return ((2 * src < cols) != (2 * to < cols)) & (to != gate(src))

    def passed(h, to):
        return send(
            panel.at[q, h], panel.at[q, h], p_send.at[h, to], c_recv.at[h, q], r, to
        )

    def middle(h):
        return cols // 2 - 1 + h

    def part_x(h, slot):
        return send(
            part_out.at[h, last],
            part_in_x.at[slot],
            b_send.at[h, last],
            x_recv.at[slot],
            r,
            middle(h),
        )

    def across_x(to, h, col):
        return send(
            panel.at[col, h], panel.at[col, h], xc_send.at[to], c_recv.at[h, col], r, to
        )

    def straight(h):
        return send(
            panel.at[last, h], grad_in.at[r], s_send, d_recv.at[r], 2 * last + h, last
        )

    def lend(h):
        return send(grad_lin.at[h], grad_x, g_send.at[h], g_recv, r, middle(h))

    def give_back(h):
        return send(norm_x, norm_back.at[h], n_send, n_recv.at[h], r, last)

    def onward(src_col, h, slot):
        to = 2 * src_col + h
        return send(
            panel.at[src_col, h], grad_in.at[slot], d_send.at[to], d_recv.at[slot], to, c
        )

    last = chip_at(chips - 1)
    side = c - middle(0)
    skips = 4 * last < cols
    central = (side >= 0) & (side < 2)
    barrier = pltpu.get_barrier_semaphore()

    def greet_row(d, _):
        pl.semaphore_signal(barrier, inc=1, device_id=(row_at(d), c), device_id_type=MESH)
        return 0

    def greet_col(d, _):
        pl.semaphore_signal(barrier, inc=1, device_id=(r, col_at(d)), device_id_type=MESH)
        return 0

    lax.fori_loop(1, rows, greet_row, 0)
    lax.fori_loop(1, cols, greet_col, 0)
    loads = [
        pltpu.make_async_copy(src, dst, load.at[n])
        for n, (src, dst) in enumerate(zip((*given, x_ref), held))
    ]
    for one in loads:
        one.start()
    for one in loads:
        one.wait()

    def spread(flat_value, dst):
        flat[...] = flat_value
        for h in range(2):
            for i in range(ti):
                dst[h, i * ti : (i + 1) * ti, :] = flat[
                    i * tj + h * ti : i * tj + (h + 1) * ti, :
                ]

    words = keep_ref[...]
    depth = words.shape[0]
    lane = lax.broadcasted_iota(jnp.int32, (depth, hidden), 1)
    pick = (lane // 16 == lax.broadcasted_iota(jnp.int32, (depth, hidden), 0)).astype(BF16)

    def by_lane(value):
        return lax.dot_general(
            value.astype(F32).astype(BF16),
            pick,
            (((0,), (0,)), ((), ())),
            preferred_element_type=F32,
        ).astype(jnp.int32)

    low = by_lane(jnp.bitwise_and(words, 255))
    high = by_lane(jnp.right_shift(words, 8))
    bit = lax.broadcasted_iota(jnp.int32, (tj, hidden), 1) % 16
    keep = jnp.bitwise_and(jnp.right_shift(low + high * 256, bit), 1).astype(F32)
    spread(
        (cot_ref[...].astype(F32).reshape(ti, tj, hidden) * keep[None]).reshape(cells, hidden)
        * (1.0 / 0.75),
        split_a,
    )

    w_left = jnp.concatenate([lp_ref[...], lg_ref[...]], axis=1)
    w_right = jnp.concatenate([rp_ref[...], rg_ref[...]], axis=1)

    def gated(x, weights):
        both = dot(x, weights)
        return both[:, :hidden], jax.nn.sigmoid(both[:, hidden:])

    pad = right_t.shape[0] // tj

    def keep_right(value, row):
        right[pl.ds(pl.multiple_of(row * cells, 8), cells), :] = value
        for j in range(ti):
            right_t[pl.ds(j, tj, stride=pad), :] = value[j * tj : (j + 1) * tj]

    def project_left(row):
        linear, sigma = gated(blocks[row], w_left)
        base = pl.multiple_of(row * cells, 8)
        left[pl.ds(base, cells), :] = (sigma * linear).astype(BF16).astype(F32)

    def other_left(d, _):
        project_left(row_at(d))
        return 0

    def project(x, row):
        linear, sigma = gated(x, w_right)
        keep_right((sigma * linear).astype(BF16).astype(F32), row)

    def zeros(count, width):
        return tuple(jnp.zeros((width, hidden), F32) for _ in range(count))

    def share(chip, h, final=False):
        accs = mac(
            zeros(ti, pad),
            tj,
            4,
            left,
            lambda i, t: r * cells + i * tj + t,
            right_t,
            lambda t: t * pad,
            pad,
        )
        for i, acc in enumerate(accs):
            wide[i * ti : (i + 1) * ti, :] = acc[:ti]

        here = middle(h) if final else chip

        @pl.when(here == c)
        def _():
            if final:
                mixed_x[...] = wide[:half, :]
            else:
                mixed[h] = wide[:half, :]

        @pl.when(here != c)
        def _():
            part_out[h, chip] = wide[:half, :].astype(BF16)

    def share_send(chip, h, final=False):
        here = middle(h) if final else chip

        @pl.when(here != c)
        def _():
            if final:
                part_x(h, c).start()
            else:
                part(h, chip, c).start()

    x = own[...]
    linear, sigma = gated(x, w_left)
    lin_a[...] = linear
    sig_a[...] = sigma
    left[pl.ds(pl.multiple_of(r * cells, 8), cells), :] = (sigma * linear).astype(BF16).astype(F32)
    linear, sigma = gated(x, w_right)
    lin_b[...] = linear
    sig_b[...] = sigma
    keep_right((sigma * linear).astype(BF16).astype(F32), r)
    share(q, core)
    spread(jax.nn.sigmoid(dot(x, og_ref[...])), split_b)
    gain = gain_ref[...]

    pl.semaphore_wait(barrier, rows - 1 + cols - 1)

    def start_first(d, _):
        first(d, r).start()
        return 0

    lax.fori_loop(1, chips, start_first, 0)
    to_sibling(x_ref, r, a_send.at[0]).start()

    share_send(q, core)

    for h in range(2):
        split_a[h] = split_a[h] * split_b[h]
        grad_lin[h] = split_a[h].astype(BF16)

    @pl.when(c == last)
    def _():
        for h in range(2):

            @pl.when(middle(h) == c)
            def _():
                grad_x[...] = grad_lin[h]

            @pl.when(middle(h) != c)
            def _():
                lend(h).start()

    def relay(d, _):
        row = 2 * chip_at(d) + core
        first(d, row).wait_recv()
        to_sibling(blocks.at[row], row, f_send.at[d]).start()
        return 0

    def direct(d, _, final=False):
        chip = chip_at(d)
        row = 2 * chip + core
        project(blocks[row], row)
        share(chip, core, final)
        share_send(chip, core, final)
        return 0

    def relayed(d, _, final=False):
        chip = chip_at(d)
        row = 2 * chip + 1 - core
        to_sibling(x_ref, row, a_send.at[0]).wait_recv()
        project(blocks[row], row)
        share(chip, 1 - core, final)
        share_send(chip, 1 - core, final)
        return 0

    relayed(0, 0)
    lax.fori_loop(1, chips - 1, relay, 0)
    lax.fori_loop(1, chips - 1, direct, 0)
    lax.fori_loop(1, chips - 1, relayed, 0)
    relay(chips - 1, 0)
    direct(chips - 1, 0, True)
    relayed(chips - 1, 0, True)

    def norm_both(value, grad_part):
        removed = value - jnp.mean(value, axis=-1, keepdims=True)
        inverse = lax.rsqrt(jnp.mean(removed * removed, axis=-1, keepdims=True) + 1e-05)
        standard = removed * inverse
        norm = dot_t(grad_part, op_ref[...]) * gain
        back = inverse * (
            norm
            - jnp.mean(norm, axis=-1, keepdims=True)
            - standard * jnp.mean(norm * standard, axis=-1, keepdims=True)
        )
        return (standard * gain).astype(BF16), back.astype(BF16)

    def norm_half(s, _):
        h = lax.rem(core + s, 2)

        def take_part(n, total):
            slot = near(n)
            part(h, slot, slot).wait_recv()
            return total + part_in[h, slot].astype(F32)

        value = lax.fori_loop(0, cols - 1, take_part, mixed[h])
        norm_back[h], panel[c, h] = norm_both(value, grad_lin[h])

        def start_across(n, _):
            to = near(cols - 2 - n)

            @pl.when((c != q) | jnp.logical_not(beyond(c, to)))
            def _():
                across(h, to, c).start()

            return 0

        lax.fori_loop(0, cols - 1, start_across, 0)
        return 0

    @pl.when(core == 1)
    def _():
        lax.fori_loop(1, rows, other_left, 0)

    @pl.when(c != last)
    def _():
        lax.fori_loop(0, 2, norm_half, 0)

    @pl.when(central)
    def _():
        @pl.when(c != last)
        def _():
            lend(side).wait_recv()

        def take_part(n, total):
            slot = near(n)
            part_x(side, slot).wait_recv()
            return total + part_in_x[slot].astype(F32)

        value = lax.fori_loop(0, cols - 1, take_part, mixed_x[...])
        normed_mix, panel[last, side] = norm_both(value, grad_x[...])

        @pl.when(c != last)
        def _():
            across_x(last, side, last).start()

        def start_across(n, _):
            to = near(cols - 2 - n)

            @pl.when(to != last)
            def _():
                across_x(to, side, last).start()

            return 0

        lax.fori_loop(0, cols - 1, start_across, 0)

        @pl.when((c != last) & skips & (side == 0))
        def _():
            straight(side).start()

        @pl.when(c == last)
        def _():
            norm_back[side] = normed_mix

        @pl.when(c != last)
        def _():
            norm_x[...] = normed_mix
            give_back(side).start()

    @pl.when(c == gate(q))
    def _():
        for s in range(2):
            h = lax.rem(core + s, 2)
            across(h, q, q).wait_recv()

            def pass_on(n, _):
                to = col_at(n)

                @pl.when(beyond(q, to))
                def _():
                    passed(h, to).start()

                return 0

            lax.fori_loop(1, cols, pass_on, 0)

    @pl.when(core == 0)
    def _():
        lax.fori_loop(1, rows, other_left, 0)

    grad_l[...] = jnp.zeros((cells, hidden), F32)

    far = beyond(q, c)

    def place_of(col):
        def seen(n, total):
            return total + jnp.where(near(n) == col, n + 1, 0)

        return lax.fori_loop(0, cols - 1, seen, 0)

    last_place = place_of(last)
    own_place = jnp.where(far, place_of(q), cols)
    low = jnp.minimum(last_place, own_place)
    high = jnp.maximum(last_place, own_place)

    def panel_at(n):
        step = lax.div(n, 2)
        turn = step + jnp.where(step >= low, 1, 0)
        turn = turn + jnp.where(turn >= high, 1, 0)
        col = jnp.where(turn == 0, c, near(turn - 1))
        at_last = jnp.where(far, cols - 2, cols - 1)
        col = jnp.where(step == at_last, last, jnp.where(step > at_last, q, col))
        return step, lax.rem(core + lax.rem(n, 2), 2), col

    def forward(n, _):
        step, h, col = panel_at(n)

        maker = jnp.where(col == last, middle(h), col)

        @pl.when((maker != c) & ((col != q) | (c != gate(q))))
        def _():
            across(h, col, col).wait_recv()

        to = 2 * col + h

        @pl.when((to != r) & jnp.logical_not(skips & (c == last) & (col == last) & (middle(h) != c) & (h == 0)))
        def _():
            onward(col, h, r).start()

        @pl.when(to == r)
        def _():
            grad_in[r] = panel[col, h]

        return 0

    def take_half(n, _):
        step, h, col = panel_at(n)
        to = 2 * col + h
        wide[:half, :] = panel[col, h].astype(F32)
        accs = mac(
            tuple(grad_l[i * tj : (i + 1) * tj, :] for i in range(ti)),
            ti,
            4,
            wide,
            lambda i, t: i * ti + t,
            right,
            lambda t: to * cells + t * tj,
            tj,
        )
        for i, acc in enumerate(accs):
            grad_l[i * tj : (i + 1) * tj, :] = acc
        return 0

    def forward_take(n, _):
        forward(n, 0)
        return take_half(n, 0)

    def take_grad(d, accs):
        row = 2 * chip_at(lax.div(d, 2)) + lax.rem(core + lax.rem(d, 2), 2)

        @pl.when(d > 0)
        def _():
            onward(c, 0, row).wait_recv()

        wide[:half, :] = grad_in[row].astype(F32)
        return mac(
            accs,
            ti,
            4,
            wide,
            lambda i, t: t * ti + i,
            left,
            lambda t: row * cells + t * tj,
            tj,
        )

    def from_gate():
        for h in range(2):

            @pl.when((c == last) & (middle(h) != c))
            def _():
                give_back(h).wait_recv()

            out_linear = dot(norm_back[h], op_ref[...])
            split_a[h] = split_a[h] * out_linear * (1.0 - split_b[h])

        for h in range(2):
            for i in range(ti):
                flat[i * tj + h * ti : i * tj + (h + 1) * ti, :] = split_a[
                    h, i * ti : (i + 1) * ti, :
                ]
        grad_gate[...] = flat[...].astype(BF16)
        total[...] = dot_t(grad_gate[...], og_ref[...])

    def some_grads(first_row, last_row):
        accs = tuple(grad_r[i * tj : (i + 1) * tj, :] for i in range(ti))
        accs = lax.fori_loop(first_row, last_row, take_grad, accs)
        for i, acc in enumerate(accs):
            grad_r[i * tj : (i + 1) * tj, :] = acc

    def from_left():
        back = gate_back(grad_l[...], lin_a[...], sig_a[...])
        return dot_t(jnp.concatenate(back, axis=1), w_left)

    def from_right():
        back = gate_back(grad_r[...], lin_b[...], sig_b[...])
        return dot_t(jnp.concatenate(back, axis=1), w_right)

    lax.fori_loop(0, 2 * cols - 2, forward_take, 0)

    inner = jnp.abs(2 * q - (chips - 1)) * 2 < chips
    soon = jnp.where(inner, 2, 2 * chips - 2)
    grad_r[...] = jnp.zeros((cells, hidden), F32)

    @pl.when(c == q)
    def _():
        from_gate()
        some_grads(0, soon)

    lax.fori_loop(2 * cols - 2, 2 * cols, forward_take, 0)

    @pl.when(c != q)
    def _():
        from_gate()
        total[...] += from_left()
        some_grads(0, rows)
        out_ref[...] = (total[...] + from_right()).astype(BF16)

    @pl.when(c == q)
    def _():
        total[...] += from_left()
        some_grads(soon, rows)
        out_ref[...] = (total[...] + from_right()).astype(BF16)

    def end_chip(d, _):
        first(d, r).wait_send()
        to_sibling(x_ref, r, f_send.at[d]).wait_send()
        return 0

    lax.fori_loop(1, chips, end_chip, 0)
    to_sibling(x_ref, r, a_send.at[0]).wait_send()

    def end_col(d, _):
        col = col_at(d)
        for h in range(2):

            @pl.when(col != last)
            def _():
                part(h, col, c).wait_send()

            @pl.when((c != last) & ((c != q) | jnp.logical_not(beyond(c, col))))
            def _():
                across(h, col, c).wait_send()

            @pl.when((c == gate(q)) & beyond(q, col))
            def _():
                passed(h, col).wait_send()

        @pl.when(central)
        def _():
            across_x(col, side, last).wait_send()

        return 0

    for h in range(2):

        @pl.when(middle(h) != c)
        def _():
            part_x(h, c).wait_send()

            @pl.when(c == last)
            def _():
                lend(h).wait_send()

    @pl.when(central & (c != last))
    def _():
        give_back(side).wait_send()

    lax.fori_loop(1, cols, end_col, 0)

    def end_row(d, _):
        to = row_at(d)
        sent = jnp.logical_not(skips) | (lax.rem(to, 2) != 0) | (c != last) | (lax.div(to, 2) != last) | (middle(lax.rem(to, 2)) == c)

        @pl.when(sent)
        def _():
            send(
                panel.at[c, 0], grad_in.at[r], d_send.at[to], d_recv.at[r], to, c
            ).wait_send()

        return 0

    @pl.when((side == 0) & (c != last) & skips)
    def _():
        straight(side).wait_send()

    lax.fori_loop(1, rows, end_row, 0)


def body(rows, cols, normed, lp, lg, rp, rg, og, op, gain, keep_bits, cotangent):
    ti, tj, width = normed.shape
    hidden = lp.shape[1]
    assert tj == 2 * ti and rows == 2 * cols
    cells = ti * tj
    half = ti * ti
    tile = pltpu.VMEM((cells, hidden), F32)
    dma = pltpu.SemaphoreType.DMA
    out = pl.pallas_call(
        functools.partial(kernel, rows, cols, ti, tj),
        out_shape=pltpu.VMEM((cells, width), BF16),
        in_specs=[pl.BlockSpec(memory_space=pl.ANY)] * 10,
        out_specs=pl.BlockSpec(memory_space=pltpu.VMEM),
        scratch_shapes=[
            *[pltpu.VMEM((width, hidden), BF16)] * 6,
            pltpu.VMEM((1, hidden), F32),
            pltpu.VMEM(keep_bits.shape[::-1], jnp.int32),
            pltpu.VMEM((cells, width), BF16),
            pltpu.VMEM((cells, width), BF16),
            pltpu.VMEM((rows, cells, width), BF16),
            pltpu.VMEM((rows * cells, hidden), F32),
            pltpu.VMEM((rows * cells, hidden), F32),
            pltpu.VMEM((tj * (-(-ti // 8) * 8), hidden), F32),
            pltpu.VMEM((2, cols, half, hidden), BF16),
            pltpu.VMEM((2, cols, half, hidden), BF16),
            pltpu.VMEM((2, half, hidden), F32),
            tile,
            pltpu.VMEM((2, half, hidden), F32),
            pltpu.VMEM((2, half, hidden), F32),
            pltpu.VMEM((cols, 2, half, hidden), BF16),
            pltpu.VMEM((rows, half, hidden), BF16),
            tile,
            tile,
            tile,
            tile,
            tile,
            tile,
            pltpu.VMEM((cells, width), BF16),
            dma((rows // 2,)),
            dma((rows // 2,)),
            dma((rows,)),
            dma((2, cols)),
            dma((2, cols)),
            dma((2, cols)),
            dma((2, cols)),
            dma((rows,)),
            dma((rows,)),
            dma((10,)),
            tile,
            tile,
            pltpu.VMEM((2, half, hidden), BF16),
            pltpu.VMEM((half, hidden), F32),
            pltpu.VMEM((cols, half, hidden), BF16),
            pltpu.VMEM((half, hidden), BF16),
            pltpu.VMEM((half, hidden), BF16),
            pltpu.VMEM((2, half, hidden), BF16),
            dma((cols,)),
            dma((2,)),
            dma,
            dma((cols,)),
            dma,
            dma((2,)),
            dma((2, cols)),
            dma,
        ],
        compiler_params=pltpu.CompilerParams(
            collective_id=0, has_side_effects=True, vmem_limit_bytes=56 * 1024 * 1024
        ),
    )(
        normed.reshape(cells, width),
        lp,
        lg,
        rp,
        rg,
        og,
        op,
        gain.reshape(1, hidden),
        keep_bits.T,
        cotangent.reshape(cells, width),
    )
    return out.reshape(ti, tj, width)


def solution(mesh):
    whole = P("row", "col", None)
    return jax.shard_map(
        functools.partial(body, mesh.shape["row"], mesh.shape["col"]),
        mesh=mesh,
        in_specs=(whole, P(), P(), P(), P(), P(), P(), P(), P("col", None), whole),
        out_specs=whole,
        check_vma=False,
    )
```

```python
import functools

import jax
import jax.numpy as jnp
from jax import lax
from jax.experimental import pallas as pl
from jax.experimental.pallas import tpu as pltpu
from jax.sharding import PartitionSpec as P

F32 = jnp.float32
BF16 = jnp.bfloat16
MESH = pl.DeviceIdType.MESH


def dot(a, b):
    return lax.dot_general(a, b, (((1,), (0,)), ((), ())), preferred_element_type=F32)


def dot_t(a, b):
    return lax.dot_general(a, b, (((1,), (1,)), ((), ())), preferred_element_type=F32)


def gate_back(grad, linear, sigma):
    part = grad * sigma
    return part.astype(BF16), (part * linear * (1.0 - sigma)).astype(BF16)


def mac(accs, steps, chunk, a_ref, a_row, b_ref, b_row, width):
    def some(block, accs):
        for u in range(chunk):
            t = block * chunk + u
            tile = b_ref[pl.ds(pl.multiple_of(b_row(t), 8), width), :]
            accs = tuple(
                acc + a_ref[pl.ds(a_row(i, t), 1), :] * tile for i, acc in enumerate(accs)
            )
        return accs

    return lax.fori_loop(0, steps // chunk, some, accs)


def kernel(
    rows,
    cols,
    ti,
    tj,
    x_ref,
    *refs,
):
    given, (out_ref, *held), scratch = refs[:9], refs[9:20], refs[20:]
    (lp_ref, lg_ref, rp_ref, rg_ref, og_ref, op_ref, gain_ref, keep_ref, cot_ref, own) = held
    (
        blocks,
        left,
        right,
        right_t,
        part_out,
        part_in,
        mixed,
        flat,
        split_a,
        split_b,
        panel,
        grad_in,
        wide,
        grad_l,
        lin_a,
        sig_a,
        lin_b,
        sig_b,
        grad_gate,
        a_send,
        f_send,
        a_recv,
        b_send,
        b_recv,
        c_send,
        c_recv,
        d_send,
        d_recv,
        load,
        grad_r,
        total,
        grad_lin,
        mixed_x,
        part_in_x,
        grad_x,
        norm_x,
        norm_back,
        x_recv,
        g_send,
        g_recv,
        xc_send,
        n_send,
        n_recv,
        p_send,
    ) = scratch
    r = lax.axis_index("row")
    c = lax.axis_index("col")
    chips = rows // 2
    q = lax.div(r, 2)
    core = lax.rem(r, 2)
    sibling = 2 * q + 1 - core
    cells = ti * tj
    half = ti * ti
    hidden = left.shape[1]

    def send(src, dst, send_sem, recv_sem, row, col):
        return pltpu.make_async_remote_copy(
            src_ref=src,
            dst_ref=dst,
            send_sem=send_sem,
            recv_sem=recv_sem,
            device_id=(row, col),
            device_id_type=MESH,
        )

    def chip_at(d):
        high = lax.rem(lax.div(q, 2) + lax.rem(d, chips // 2), chips // 2)
        return 2 * high + lax.rem(lax.rem(q, 2) + lax.div(d, chips // 2), 2)

    def row_at(d):
        return lax.rem(r + d, rows)

    def col_at(d):
        return lax.rem(c + d, cols)

    def first(d, src_row):
        to = 2 * chip_at(d) + core
        return send(x_ref, blocks.at[src_row], a_send.at[d], a_recv.at[src_row], to, c)

    def to_sibling(src, src_row, sem):
        return send(src, blocks.at[src_row], sem, a_recv.at[src_row], sibling, c)

    def near(n):
        least = jnp.minimum(c, cols - 1 - c)
        both = (lax.div(n, 2) + 1) * (1 - 2 * lax.rem(n, 2))
        longer = (n - least + 1) * jnp.where(2 * c < cols, 1, -1)
        return c + jnp.where(n < 2 * least, both, longer)

    def part(h, to, slot):
        return send(
            part_out.at[h, to], part_in.at[h, slot], b_send.at[h, to], b_recv.at[h, slot], r, to
        )

    def across(h, to, slot):
        return send(
            panel.at[c, h], panel.at[slot, h], c_send.at[h, to], c_recv.at[h, slot], r, to
        )

    def gate(src):
        return jnp.where(2 * src < cols, cols // 2, cols // 2 - 1)

    def beyond(src, to):
        return ((2 * src < cols) != (2 * to < cols)) & (to != gate(src))

    def passed(h, to):
        return send(
            panel.at[q, h], panel.at[q, h], p_send.at[h, to], c_recv.at[h, q], r, to
        )

    def middle(h):
        return cols // 2 - 1 + h

    def part_x(h, slot):
        return send(
            part_out.at[h, last],
            part_in_x.at[slot],
            b_send.at[h, last],
            x_recv.at[slot],
            r,
            middle(h),
        )

    def across_x(to, h, col):
        return send(
            panel.at[col, h], panel.at[col, h], xc_send.at[to], c_recv.at[h, col], r, to
        )

    def lend(h):
        return send(grad_lin.at[h], grad_x, g_send.at[h], g_recv, r, middle(h))

    def give_back(h):
        return send(norm_x, norm_back.at[h], n_send, n_recv.at[h], r, last)

    def onward(src_col, h, slot):
        to = 2 * src_col + h
        return send(
            panel.at[src_col, h], grad_in.at[slot], d_send.at[to], d_recv.at[slot], to, c
        )

    last = chip_at(chips - 1)
    side = c - middle(0)
    central = (side >= 0) & (side < 2)
    barrier = pltpu.get_barrier_semaphore()

    def greet_row(d, _):
        pl.semaphore_signal(barrier, inc=1, device_id=(row_at(d), c), device_id_type=MESH)
        return 0

    def greet_col(d, _):
        pl.semaphore_signal(barrier, inc=1, device_id=(r, col_at(d)), device_id_type=MESH)
        return 0

    lax.fori_loop(1, rows, greet_row, 0)
    lax.fori_loop(1, cols, greet_col, 0)
    loads = [
        pltpu.make_async_copy(src, dst, load.at[n])
        for n, (src, dst) in enumerate(zip((*given, x_ref), held))
    ]
    for one in loads:
        one.start()
    for one in loads:
        one.wait()

    def spread(flat_value, dst):
        flat[...] = flat_value
        for h in range(2):
            for i in range(ti):
                dst[h, i * ti : (i + 1) * ti, :] = flat[
                    i * tj + h * ti : i * tj + (h + 1) * ti, :
                ]

    words = keep_ref[...]
    depth = words.shape[0]
    lane = lax.broadcasted_iota(jnp.int32, (depth, hidden), 1)
    pick = (lane // 16 == lax.broadcasted_iota(jnp.int32, (depth, hidden), 0)).astype(BF16)

    def by_lane(value):
        return lax.dot_general(
            value.astype(F32).astype(BF16),
            pick,
            (((0,), (0,)), ((), ())),
            preferred_element_type=F32,
        ).astype(jnp.int32)

    low = by_lane(jnp.bitwise_and(words, 255))
    high = by_lane(jnp.right_shift(words, 8))
    bit = lax.broadcasted_iota(jnp.int32, (tj, hidden), 1) % 16
    keep = jnp.bitwise_and(jnp.right_shift(low + high * 256, bit), 1).astype(F32)
    spread(
        (cot_ref[...].astype(F32).reshape(ti, tj, hidden) * keep[None]).reshape(cells, hidden)
        * (1.0 / 0.75),
        split_a,
    )

    w_left = jnp.concatenate([lp_ref[...], lg_ref[...]], axis=1)
    w_right = jnp.concatenate([rp_ref[...], rg_ref[...]], axis=1)

    def gated(x, weights):
        both = dot(x, weights)
        return both[:, :hidden], jax.nn.sigmoid(both[:, hidden:])

    pad = right_t.shape[0] // tj

    def keep_right(value, row):
        right[pl.ds(pl.multiple_of(row * cells, 8), cells), :] = value
        for j in range(ti):
            right_t[pl.ds(j, tj, stride=pad), :] = value[j * tj : (j + 1) * tj]

    def project_left(row):
        linear, sigma = gated(blocks[row], w_left)
        base = pl.multiple_of(row * cells, 8)
        left[pl.ds(base, cells), :] = (sigma * linear).astype(BF16).astype(F32)

    def other_left(d, _):
        project_left(row_at(d))
        return 0

    def project(x, row):
        linear, sigma = gated(x, w_right)
        keep_right((sigma * linear).astype(BF16).astype(F32), row)

    def zeros(count, width):
        return tuple(jnp.zeros((width, hidden), F32) for _ in range(count))

    def share(chip, h, final=False):
        accs = mac(
            zeros(ti, pad),
            tj,
            4,
            left,
            lambda i, t: r * cells + i * tj + t,
            right_t,
            lambda t: t * pad,
            pad,
        )
        for i, acc in enumerate(accs):
            wide[i * ti : (i + 1) * ti, :] = acc[:ti]

        here = middle(h) if final else chip

        @pl.when(here == c)
        def _():
            if final:
                mixed_x[...] = wide[:half, :]
            else:
                mixed[h] = wide[:half, :]

        @pl.when(here != c)
        def _():
            part_out[h, chip] = wide[:half, :].astype(BF16)

    def share_send(chip, h, final=False):
        here = middle(h) if final else chip

        @pl.when(here != c)
        def _():
            if final:
                part_x(h, c).start()
            else:
                part(h, chip, c).start()

    x = own[...]
    linear, sigma = gated(x, w_left)
    lin_a[...] = linear
    sig_a[...] = sigma
    left[pl.ds(pl.multiple_of(r * cells, 8), cells), :] = (sigma * linear).astype(BF16).astype(F32)
    linear, sigma = gated(x, w_right)
    lin_b[...] = linear
    sig_b[...] = sigma
    keep_right((sigma * linear).astype(BF16).astype(F32), r)
    share(q, core)
    spread(jax.nn.sigmoid(dot(x, og_ref[...])), split_b)
    gain = gain_ref[...]

    pl.semaphore_wait(barrier, rows - 1 + cols - 1)

    def start_first(d, _):
        first(d, r).start()
        return 0

    lax.fori_loop(1, chips, start_first, 0)
    to_sibling(x_ref, r, a_send.at[0]).start()

    share_send(q, core)

    for h in range(2):
        split_a[h] = split_a[h] * split_b[h]
        grad_lin[h] = split_a[h].astype(BF16)

    @pl.when(c == last)
    def _():
        for h in range(2):

            @pl.when(middle(h) == c)
            def _():
                grad_x[...] = grad_lin[h]

            @pl.when(middle(h) != c)
            def _():
                lend(h).start()

    def relay(d, _):
        row = 2 * chip_at(d) + core
        first(d, row).wait_recv()
        to_sibling(blocks.at[row], row, f_send.at[d]).start()
        return 0

    def direct(d, _, final=False):
        chip = chip_at(d)
        row = 2 * chip + core
        project(blocks[row], row)
        share(chip, core, final)
        share_send(chip, core, final)
        return 0

    def relayed(d, _, final=False):
        chip = chip_at(d)
        row = 2 * chip + 1 - core
        to_sibling(x_ref, row, a_send.at[0]).wait_recv()
        project(blocks[row], row)
        share(chip, 1 - core, final)
        share_send(chip, 1 - core, final)
        return 0

    relayed(0, 0)
    lax.fori_loop(1, chips - 1, relay, 0)
    lax.fori_loop(1, chips - 1, direct, 0)
    lax.fori_loop(1, chips - 1, relayed, 0)
    relay(chips - 1, 0)
    direct(chips - 1, 0, True)
    relayed(chips - 1, 0, True)

    def norm_both(value, grad_part):
        removed = value - jnp.mean(value, axis=-1, keepdims=True)
        inverse = lax.rsqrt(jnp.mean(removed * removed, axis=-1, keepdims=True) + 1e-05)
        standard = removed * inverse
        norm = dot_t(grad_part, op_ref[...]) * gain
        back = inverse * (
            norm
            - jnp.mean(norm, axis=-1, keepdims=True)
            - standard * jnp.mean(norm * standard, axis=-1, keepdims=True)
        )
        return (standard * gain).astype(BF16), back.astype(BF16)

    def norm_half(s, _):
        h = lax.rem(core + s, 2)

        def take_part(n, total):
            slot = near(n)
            part(h, slot, slot).wait_recv()
            return total + part_in[h, slot].astype(F32)

        value = lax.fori_loop(0, cols - 1, take_part, mixed[h])
        norm_back[h], panel[c, h] = norm_both(value, grad_lin[h])

        def start_across(n, _):
            to = jnp.where((2 * c == cols - 2) & (n > 0), near(n - 1), near(cols - 2 - n))

            @pl.when((c != q) | jnp.logical_not(beyond(c, to)))
            def _():
                across(h, to, c).start()

            return 0

        lax.fori_loop(0, cols - 1, start_across, 0)
        return 0

    @pl.when(c == last)
    def _():
        lax.fori_loop(1, rows, other_left, 0)

    @pl.when(c != last)
    def _():
        lax.fori_loop(0, 2, norm_half, 0)

    @pl.when(central)
    def _():
        @pl.when(c != last)
        def _():
            lend(side).wait_recv()

        def take_part(n, total):
            slot = near(n)
            part_x(side, slot).wait_recv()
            return total + part_in_x[slot].astype(F32)

        value = lax.fori_loop(0, cols - 1, take_part, mixed_x[...])
        normed_mix, panel[last, side] = norm_both(value, grad_x[...])

        @pl.when(c != last)
        def _():
            across_x(last, side, last).start()

        def start_across(n, _):
            to = near(cols - 2 - n)

            @pl.when(to != last)
            def _():
                across_x(to, side, last).start()

            return 0

        lax.fori_loop(0, cols - 1, start_across, 0)

        @pl.when(c == last)
        def _():
            norm_back[side] = normed_mix

        @pl.when(c != last)
        def _():
            norm_x[...] = normed_mix
            give_back(side).start()

    @pl.when(c == gate(q))
    def _():
        for s in range(2):
            h = lax.rem(core + s, 2)
            across(h, q, q).wait_recv()

            def pass_on(n, _):
                to = col_at(n)

                @pl.when(beyond(q, to))
                def _():
                    passed(h, to).start()

                return 0

            lax.fori_loop(1, cols, pass_on, 0)

    @pl.when(c != last)
    def _():
        lax.fori_loop(1, rows, other_left, 0)

    grad_l[...] = jnp.zeros((cells, hidden), F32)

    far = beyond(q, c)

    def place_of(col):
        def seen(n, total):
            return total + jnp.where(near(n) == col, n + 1, 0)

        return lax.fori_loop(0, cols - 1, seen, 0)

    last_place = place_of(last)
    own_place = jnp.where(far, place_of(q), cols)
    low = jnp.minimum(last_place, own_place)
    high = jnp.maximum(last_place, own_place)

    def panel_at(n):
        step = lax.div(n, 2)
        turn = step + jnp.where(step >= low, 1, 0)
        turn = turn + jnp.where(turn >= high, 1, 0)
        col = jnp.where(turn == 0, c, near(turn - 1))
        at_last = jnp.where(far, cols - 2, cols - 1)
        col = jnp.where(step == at_last, last, jnp.where(step > at_last, q, col))
        return step, lax.rem(core + lax.rem(n, 2), 2), col

    def forward(n, _):
        step, h, col = panel_at(n)

        maker = jnp.where(col == last, middle(h), col)

        @pl.when((maker != c) & ((col != q) | (c != gate(q))))
        def _():
            across(h, col, col).wait_recv()

        to = 2 * col + h

        @pl.when(to != r)
        def _():
            onward(col, h, r).start()

        @pl.when(to == r)
        def _():
            grad_in[r] = panel[col, h]

        return 0

    def take_half(n, _):
        step, h, col = panel_at(n)
        to = 2 * col + h
        wide[:half, :] = panel[col, h].astype(F32)
        accs = mac(
            tuple(grad_l[i * tj : (i + 1) * tj, :] for i in range(ti)),
            ti,
            4,
            wide,
            lambda i, t: i * ti + t,
            right,
            lambda t: to * cells + t * tj,
            tj,
        )
        for i, acc in enumerate(accs):
            grad_l[i * tj : (i + 1) * tj, :] = acc
        return 0

    def forward_take(n, _):
        forward(n, 0)
        return take_half(n, 0)

    def take_grad(d, accs):
        row = 2 * chip_at(lax.div(d, 2)) + lax.rem(core + lax.rem(d, 2), 2)

        @pl.when(d > 0)
        def _():
            onward(c, 0, row).wait_recv()

        wide[:half, :] = grad_in[row].astype(F32)
        return mac(
            accs,
            ti,
            4,
            wide,
            lambda i, t: t * ti + i,
            left,
            lambda t: row * cells + t * tj,
            tj,
        )

    def from_gate():
        for h in range(2):

            @pl.when((c == last) & (middle(h) != c))
            def _():
                give_back(h).wait_recv()

            out_linear = dot(norm_back[h], op_ref[...])
            split_a[h] = split_a[h] * out_linear * (1.0 - split_b[h])

        for h in range(2):
            for i in range(ti):
                flat[i * tj + h * ti : i * tj + (h + 1) * ti, :] = split_a[
                    h, i * ti : (i + 1) * ti, :
                ]
        grad_gate[...] = flat[...].astype(BF16)
        total[...] = dot_t(grad_gate[...], og_ref[...])

    def some_grads(first_row, last_row):
        accs = tuple(grad_r[i * tj : (i + 1) * tj, :] for i in range(ti))
        accs = lax.fori_loop(first_row, last_row, take_grad, accs)
        for i, acc in enumerate(accs):
            grad_r[i * tj : (i + 1) * tj, :] = acc

    def from_left():
        back = gate_back(grad_l[...], lin_a[...], sig_a[...])
        return dot_t(jnp.concatenate(back, axis=1), w_left)

    def from_right():
        back = gate_back(grad_r[...], lin_b[...], sig_b[...])
        return dot_t(jnp.concatenate(back, axis=1), w_right)

    lax.fori_loop(0, 2 * cols - 2, forward_take, 0)

    inner = jnp.abs(2 * q - (chips - 1)) * 2 < chips
    soon = jnp.where(inner, 2, 2 * chips - 2)
    grad_r[...] = jnp.zeros((cells, hidden), F32)

    @pl.when(c == q)
    def _():
        from_gate()
        some_grads(0, soon)

    lax.fori_loop(2 * cols - 2, 2 * cols, forward_take, 0)

    @pl.when(c != q)
    def _():
        from_gate()
        total[...] += from_left()
        some_grads(0, rows)
        out_ref[...] = (total[...] + from_right()).astype(BF16)

    @pl.when(c == q)
    def _():
        total[...] += from_left()
        some_grads(soon, rows)
        out_ref[...] = (total[...] + from_right()).astype(BF16)

    def end_chip(d, _):
        first(d, r).wait_send()
        to_sibling(x_ref, r, f_send.at[d]).wait_send()
        return 0

    lax.fori_loop(1, chips, end_chip, 0)
    to_sibling(x_ref, r, a_send.at[0]).wait_send()

    def end_col(d, _):
        col = col_at(d)
        for h in range(2):

            @pl.when(col != last)
            def _():
                part(h, col, c).wait_send()

            @pl.when((c != last) & ((c != q) | jnp.logical_not(beyond(c, col))))
            def _():
                across(h, col, c).wait_send()

            @pl.when((c == gate(q)) & beyond(q, col))
            def _():
                passed(h, col).wait_send()

        @pl.when(central)
        def _():
            across_x(col, side, last).wait_send()

        return 0

    for h in range(2):

        @pl.when(middle(h) != c)
        def _():
            part_x(h, c).wait_send()

            @pl.when(c == last)
            def _():
                lend(h).wait_send()

    @pl.when(central & (c != last))
    def _():
        give_back(side).wait_send()

    lax.fori_loop(1, cols, end_col, 0)

    def end_row(d, _):
        to = row_at(d)
        send(
            panel.at[c, 0], grad_in.at[r], d_send.at[to], d_recv.at[r], to, c
        ).wait_send()
        return 0

    lax.fori_loop(1, rows, end_row, 0)


def body(rows, cols, normed, lp, lg, rp, rg, og, op, gain, keep_bits, cotangent):
    ti, tj, width = normed.shape
    hidden = lp.shape[1]
    assert tj == 2 * ti and rows == 2 * cols
    cells = ti * tj
    half = ti * ti
    tile = pltpu.VMEM((cells, hidden), F32)
    dma = pltpu.SemaphoreType.DMA
    out = pl.pallas_call(
        functools.partial(kernel, rows, cols, ti, tj),
        out_shape=pltpu.VMEM((cells, width), BF16),
        in_specs=[pl.BlockSpec(memory_space=pl.ANY)] * 10,
        out_specs=pl.BlockSpec(memory_space=pltpu.VMEM),
        scratch_shapes=[
            *[pltpu.VMEM((width, hidden), BF16)] * 6,
            pltpu.VMEM((1, hidden), F32),
            pltpu.VMEM(keep_bits.shape[::-1], jnp.int32),
            pltpu.VMEM((cells, width), BF16),
            pltpu.VMEM((cells, width), BF16),
            pltpu.VMEM((rows, cells, width), BF16),
            pltpu.VMEM((rows * cells, hidden), F32),
            pltpu.VMEM((rows * cells, hidden), F32),
            pltpu.VMEM((tj * (-(-ti // 8) * 8), hidden), F32),
            pltpu.VMEM((2, cols, half, hidden), BF16),
            pltpu.VMEM((2, cols, half, hidden), BF16),
            pltpu.VMEM((2, half, hidden), F32),
            tile,
            pltpu.VMEM((2, half, hidden), F32),
            pltpu.VMEM((2, half, hidden), F32),
            pltpu.VMEM((cols, 2, half, hidden), BF16),
            pltpu.VMEM((rows, half, hidden), BF16),
            tile,
            tile,
            tile,
            tile,
            tile,
            tile,
            pltpu.VMEM((cells, width), BF16),
            dma((rows // 2,)),
            dma((rows // 2,)),
            dma((rows,)),
            dma((2, cols)),
            dma((2, cols)),
            dma((2, cols)),
            dma((2, cols)),
            dma((rows,)),
            dma((rows,)),
            dma((10,)),
            tile,
            tile,
            pltpu.VMEM((2, half, hidden), BF16),
            pltpu.VMEM((half, hidden), F32),
            pltpu.VMEM((cols, half, hidden), BF16),
            pltpu.VMEM((half, hidden), BF16),
            pltpu.VMEM((half, hidden), BF16),
            pltpu.VMEM((2, half, hidden), BF16),
            dma((cols,)),
            dma((2,)),
            dma,
            dma((cols,)),
            dma,
            dma((2,)),
            dma((2, cols)),
        ],
        compiler_params=pltpu.CompilerParams(
            collective_id=0, has_side_effects=True, vmem_limit_bytes=56 * 1024 * 1024
        ),
    )(
        normed.reshape(cells, width),
        lp,
        lg,
        rp,
        rg,
        og,
        op,
        gain.reshape(1, hidden),
        keep_bits.T,
        cotangent.reshape(cells, width),
    )
    return out.reshape(ti, tj, width)


def solution(mesh):
    whole = P("row", "col", None)
    return jax.shard_map(
        functools.partial(body, mesh.shape["row"], mesh.shape["col"]),
        mesh=mesh,
        in_specs=(whole, P(), P(), P(), P(), P(), P(), P(), P("col", None), whole),
        out_specs=whole,
        check_vma=False,
    )
```

```python
import functools

import jax
import jax.numpy as jnp
from jax import lax
from jax.experimental import pallas as pl
from jax.experimental.pallas import tpu as pltpu
from jax.sharding import PartitionSpec as P

F32 = jnp.float32
BF16 = jnp.bfloat16
MESH = pl.DeviceIdType.MESH


def dot(a, b):
    return lax.dot_general(a, b, (((1,), (0,)), ((), ())), preferred_element_type=F32)


def dot_t(a, b):
    return lax.dot_general(a, b, (((1,), (1,)), ((), ())), preferred_element_type=F32)


def gate_back(grad, linear, sigma):
    part = grad * sigma
    return part.astype(BF16), (part * linear * (1.0 - sigma)).astype(BF16)


def mac(accs, steps, chunk, a_ref, a_row, b_ref, b_row, width):
    def some(block, accs):
        for u in range(chunk):
            t = block * chunk + u
            tile = b_ref[pl.ds(pl.multiple_of(b_row(t), 8), width), :]
            accs = tuple(
                acc + a_ref[pl.ds(a_row(i, t), 1), :] * tile for i, acc in enumerate(accs)
            )
        return accs

    return lax.fori_loop(0, steps // chunk, some, accs)


def kernel(
    rows,
    cols,
    ti,
    tj,
    x_ref,
    *refs,
):
    given, (out_ref, *held), scratch = refs[:9], refs[9:20], refs[20:]
    (lp_ref, lg_ref, rp_ref, rg_ref, og_ref, op_ref, gain_ref, keep_ref, cot_ref, own) = held
    (
        blocks,
        left,
        right,
        right_t,
        part_out,
        part_in,
        mixed,
        flat,
        split_a,
        split_b,
        panel,
        grad_in,
        wide,
        grad_l,
        lin_a,
        sig_a,
        lin_b,
        sig_b,
        grad_gate,
        a_send,
        f_send,
        a_recv,
        b_send,
        b_recv,
        c_send,
        c_recv,
        d_send,
        d_recv,
        load,
        grad_r,
        total,
        grad_lin,
        mixed_x,
        part_in_x,
        grad_x,
        norm_x,
        norm_back,
        x_recv,
        g_send,
        g_recv,
        xc_send,
        n_send,
        n_recv,
        p_send,
    ) = scratch
    r = lax.axis_index("row")
    c = lax.axis_index("col")
    chips = rows // 2
    q = lax.div(r, 2)
    core = lax.rem(r, 2)
    sibling = 2 * q + 1 - core
    cells = ti * tj
    half = ti * ti
    hidden = left.shape[1]

    def send(src, dst, send_sem, recv_sem, row, col):
        return pltpu.make_async_remote_copy(
            src_ref=src,
            dst_ref=dst,
            send_sem=send_sem,
            recv_sem=recv_sem,
            device_id=(row, col),
            device_id_type=MESH,
        )

    def chip_at(d):
        high = lax.rem(lax.div(q, 2) + lax.rem(d, chips // 2), chips // 2)
        return 2 * high + lax.rem(lax.rem(q, 2) + lax.div(d, chips // 2), 2)

    def row_at(d):
        return lax.rem(r + d, rows)

    def col_at(d):
        return lax.rem(c + d, cols)

    def first(d, src_row):
        to = 2 * chip_at(d) + core
        return send(x_ref, blocks.at[src_row], a_send.at[d], a_recv.at[src_row], to, c)

    def to_sibling(src, src_row, sem):
        return send(src, blocks.at[src_row], sem, a_recv.at[src_row], sibling, c)

    def near(n):
        least = jnp.minimum(c, cols - 1 - c)
        both = (lax.div(n, 2) + 1) * (1 - 2 * lax.rem(n, 2))
        longer = (n - least + 1) * jnp.where(2 * c < cols, 1, -1)
        return c + jnp.where(n < 2 * least, both, longer)

    def part(h, to, slot):
        return send(
            part_out.at[h, to], part_in.at[h, slot], b_send.at[h, to], b_recv.at[h, slot], r, to
        )

    def across(h, to, slot):
        return send(
            panel.at[c, h], panel.at[slot, h], c_send.at[h, to], c_recv.at[h, slot], r, to
        )

    def gate(src):
        return jnp.where(2 * src < cols, cols // 2, cols // 2 - 1)

    def beyond(src, to):
        return ((2 * src < cols) != (2 * to < cols)) & (to != gate(src))

    def passed(h, to):
        return send(
            panel.at[q, h], panel.at[q, h], p_send.at[h, to], c_recv.at[h, q], r, to
        )

    def middle(h):
        return cols // 2 - 1 + h

    def part_x(h, slot):
        return send(
            part_out.at[h, last],
            part_in_x.at[slot],
            b_send.at[h, last],
            x_recv.at[slot],
            r,
            middle(h),
        )

    def across_x(to, h, col):
        return send(
            panel.at[col, h], panel.at[col, h], xc_send.at[to], c_recv.at[h, col], r, to
        )

    def lend(h):
        return send(grad_lin.at[h], grad_x, g_send.at[h], g_recv, r, middle(h))

    def give_back(h):
        return send(norm_x, norm_back.at[h], n_send, n_recv.at[h], r, last)

    def onward(src_col, h, slot):
        to = 2 * src_col + h
        return send(
            panel.at[src_col, h], grad_in.at[slot], d_send.at[to], d_recv.at[slot], to, c
        )

    last = chip_at(chips - 1)
    side = c - middle(0)
    central = (side >= 0) & (side < 2)
    barrier = pltpu.get_barrier_semaphore()

    def greet_row(d, _):
        pl.semaphore_signal(barrier, inc=1, device_id=(row_at(d), c), device_id_type=MESH)
        return 0

    def greet_col(d, _):
        pl.semaphore_signal(barrier, inc=1, device_id=(r, col_at(d)), device_id_type=MESH)
        return 0

    lax.fori_loop(1, rows, greet_row, 0)
    lax.fori_loop(1, cols, greet_col, 0)
    loads = [
        pltpu.make_async_copy(src, dst, load.at[n])
        for n, (src, dst) in enumerate(zip((*given, x_ref), held))
    ]
    for one in loads:
        one.start()
    for one in loads:
        one.wait()

    def spread(flat_value, dst):
        flat[...] = flat_value
        for h in range(2):
            for i in range(ti):
                dst[h, i * ti : (i + 1) * ti, :] = flat[
                    i * tj + h * ti : i * tj + (h + 1) * ti, :
                ]

    words = keep_ref[...]
    depth = words.shape[0]
    lane = lax.broadcasted_iota(jnp.int32, (depth, hidden), 1)
    pick = (lane // 16 == lax.broadcasted_iota(jnp.int32, (depth, hidden), 0)).astype(BF16)

    def by_lane(value):
        return lax.dot_general(
            value.astype(F32).astype(BF16),
            pick,
            (((0,), (0,)), ((), ())),
            preferred_element_type=F32,
        ).astype(jnp.int32)

    low = by_lane(jnp.bitwise_and(words, 255))
    high = by_lane(jnp.right_shift(words, 8))
    bit = lax.broadcasted_iota(jnp.int32, (tj, hidden), 1) % 16
    keep = jnp.bitwise_and(jnp.right_shift(low + high * 256, bit), 1).astype(F32)
    spread(
        (cot_ref[...].astype(F32).reshape(ti, tj, hidden) * keep[None]).reshape(cells, hidden)
        * (1.0 / 0.75),
        split_a,
    )

    w_left = jnp.concatenate([lp_ref[...], lg_ref[...]], axis=1)
    w_right = jnp.concatenate([rp_ref[...], rg_ref[...]], axis=1)

    def gated(x, weights):
        both = dot(x, weights)
        return both[:, :hidden], jax.nn.sigmoid(both[:, hidden:])

    pad = right_t.shape[0] // tj

    def keep_right(value, row):
        right[pl.ds(pl.multiple_of(row * cells, 8), cells), :] = value
        for j in range(ti):
            right_t[pl.ds(j, tj, stride=pad), :] = value[j * tj : (j + 1) * tj]

    def project_left(row):
        linear, sigma = gated(blocks[row], w_left)
        base = pl.multiple_of(row * cells, 8)
        left[pl.ds(base, cells), :] = (sigma * linear).astype(BF16).astype(F32)

    def other_left(d, _):
        project_left(row_at(d))
        return 0

    def project(x, row):
        linear, sigma = gated(x, w_right)
        keep_right((sigma * linear).astype(BF16).astype(F32), row)

    def zeros(count, width):
        return tuple(jnp.zeros((width, hidden), F32) for _ in range(count))

    def share(chip, h, final=False):
        accs = mac(
            zeros(ti, pad),
            tj,
            8,
            left,
            lambda i, t: r * cells + i * tj + t,
            right_t,
            lambda t: t * pad,
            pad,
        )
        for i, acc in enumerate(accs):
            wide[i * ti : (i + 1) * ti, :] = acc[:ti]

        here = middle(h) if final else chip

        @pl.when(here == c)
        def _():
            if final:
                mixed_x[...] = wide[:half, :]
            else:
                mixed[h] = wide[:half, :]

        @pl.when(here != c)
        def _():
            part_out[h, chip] = wide[:half, :].astype(BF16)

    def share_send(chip, h, final=False):
        here = middle(h) if final else chip

        @pl.when(here != c)
        def _():
            if final:
                part_x(h, c).start()
            else:
                part(h, chip, c).start()

    x = own[...]
    linear, sigma = gated(x, w_left)
    lin_a[...] = linear
    sig_a[...] = sigma
    left[pl.ds(pl.multiple_of(r * cells, 8), cells), :] = (sigma * linear).astype(BF16).astype(F32)
    linear, sigma = gated(x, w_right)
    lin_b[...] = linear
    sig_b[...] = sigma
    keep_right((sigma * linear).astype(BF16).astype(F32), r)
    share(q, core)
    spread(jax.nn.sigmoid(dot(x, og_ref[...])), split_b)
    gain = gain_ref[...]

    pl.semaphore_wait(barrier, rows - 1 + cols - 1)

    def start_first(d, _):
        first(d, r).start()
        return 0

    lax.fori_loop(1, chips, start_first, 0)
    to_sibling(x_ref, r, a_send.at[0]).start()

    share_send(q, core)

    for h in range(2):
        split_a[h] = split_a[h] * split_b[h]
        grad_lin[h] = split_a[h].astype(BF16)

    @pl.when(c == last)
    def _():
        for h in range(2):

            @pl.when(middle(h) == c)
            def _():
                grad_x[...] = grad_lin[h]

            @pl.when(middle(h) != c)
            def _():
                lend(h).start()

    def relay(d, _):
        row = 2 * chip_at(d) + core
        first(d, row).wait_recv()
        to_sibling(blocks.at[row], row, f_send.at[d]).start()
        return 0

    def direct(d, _, final=False):
        chip = chip_at(d)
        row = 2 * chip + core
        project(blocks[row], row)
        share(chip, core, final)
        share_send(chip, core, final)
        return 0

    def relayed(d, _, final=False):
        chip = chip_at(d)
        row = 2 * chip + 1 - core
        to_sibling(x_ref, row, a_send.at[0]).wait_recv()
        project(blocks[row], row)
        share(chip, 1 - core, final)
        share_send(chip, 1 - core, final)
        return 0

    relayed(0, 0)
    lax.fori_loop(1, chips - 1, relay, 0)
    lax.fori_loop(1, chips - 1, direct, 0)
    lax.fori_loop(1, chips - 1, relayed, 0)
    relay(chips - 1, 0)
    direct(chips - 1, 0, True)
    relayed(chips - 1, 0, True)

    def norm_both(value, grad_part):
        removed = value - jnp.mean(value, axis=-1, keepdims=True)
        inverse = lax.rsqrt(jnp.mean(removed * removed, axis=-1, keepdims=True) + 1e-05)
        standard = removed * inverse
        norm = dot_t(grad_part, op_ref[...]) * gain
        back = inverse * (
            norm
            - jnp.mean(norm, axis=-1, keepdims=True)
            - standard * jnp.mean(norm * standard, axis=-1, keepdims=True)
        )
        return (standard * gain).astype(BF16), back.astype(BF16)

    def norm_half(s, _):
        h = lax.rem(core + s, 2)

        def take_part(n, total):
            slot = near(n)
            part(h, slot, slot).wait_recv()
            return total + part_in[h, slot].astype(F32)

        value = lax.fori_loop(0, cols - 1, take_part, mixed[h])
        norm_back[h], panel[c, h] = norm_both(value, grad_lin[h])

        def start_across(n, _):
            to = jnp.where((2 * c == cols - 2) & (n > 0), near(n - 1), near(cols - 2 - n))

            @pl.when((c != q) | jnp.logical_not(beyond(c, to)))
            def _():
                across(h, to, c).start()

            return 0

        lax.fori_loop(0, cols - 1, start_across, 0)
        return 0

    @pl.when(c == last)
    def _():
        lax.fori_loop(1, rows, other_left, 0)

    @pl.when(c != last)
    def _():
        lax.fori_loop(0, 2, norm_half, 0)

    @pl.when(central)
    def _():
        @pl.when(c != last)
        def _():
            lend(side).wait_recv()

        def take_part(n, total):
            slot = near(n)
            part_x(side, slot).wait_recv()
            return total + part_in_x[slot].astype(F32)

        value = lax.fori_loop(0, cols - 1, take_part, mixed_x[...])
        normed_mix, panel[last, side] = norm_both(value, grad_x[...])

        @pl.when(c != last)
        def _():
            across_x(last, side, last).start()

        def start_across(n, _):
            to = near(cols - 2 - n)

            @pl.when(to != last)
            def _():
                across_x(to, side, last).start()

            return 0

        lax.fori_loop(0, cols - 1, start_across, 0)

        @pl.when(c == last)
        def _():
            norm_back[side] = normed_mix

        @pl.when(c != last)
        def _():
            norm_x[...] = normed_mix
            give_back(side).start()

    @pl.when(c == gate(q))
    def _():
        for s in range(2):
            h = lax.rem(core + s, 2)
            across(h, q, q).wait_recv()

            def pass_on(n, _):
                to = col_at(n)

                @pl.when(beyond(q, to))
                def _():
                    passed(h, to).start()

                return 0

            lax.fori_loop(1, cols, pass_on, 0)

    @pl.when(c != last)
    def _():
        lax.fori_loop(1, rows, other_left, 0)

    grad_l[...] = jnp.zeros((cells, hidden), F32)

    far = beyond(q, c)

    def place_of(col):
        def seen(n, total):
            return total + jnp.where(near(n) == col, n + 1, 0)

        return lax.fori_loop(0, cols - 1, seen, 0)

    last_place = place_of(last)
    own_place = jnp.where(far, place_of(q), cols)
    low = jnp.minimum(last_place, own_place)
    high = jnp.maximum(last_place, own_place)

    def panel_at(n):
        step = lax.div(n, 2)
        turn = step + jnp.where(step >= low, 1, 0)
        turn = turn + jnp.where(turn >= high, 1, 0)
        col = jnp.where(turn == 0, c, near(turn - 1))
        at_last = jnp.where(far, cols - 2, cols - 1)
        col = jnp.where(step == at_last, last, jnp.where(step > at_last, q, col))
        return step, lax.rem(core + lax.rem(n, 2), 2), col

    def forward(n, _):
        step, h, col = panel_at(n)

        maker = jnp.where(col == last, middle(h), col)

        @pl.when((maker != c) & ((col != q) | (c != gate(q))))
        def _():
            across(h, col, col).wait_recv()

        to = 2 * col + h

        @pl.when(to != r)
        def _():
            onward(col, h, r).start()

        @pl.when(to == r)
        def _():
            grad_in[r] = panel[col, h]

        return 0

    def take_half(n, _):
        step, h, col = panel_at(n)
        to = 2 * col + h
        wide[:half, :] = panel[col, h].astype(F32)
        accs = mac(
            tuple(grad_l[i * tj : (i + 1) * tj, :] for i in range(ti)),
            ti,
            6,
            wide,
            lambda i, t: i * ti + t,
            right,
            lambda t: to * cells + t * tj,
            tj,
        )
        for i, acc in enumerate(accs):
            grad_l[i * tj : (i + 1) * tj, :] = acc
        return 0

    def forward_take(n, _):
        forward(n, 0)
        return take_half(n, 0)

    def take_grad(d, accs):
        row = 2 * chip_at(lax.div(d, 2)) + lax.rem(core + lax.rem(d, 2), 2)

        @pl.when(d > 0)
        def _():
            onward(c, 0, row).wait_recv()

        wide[:half, :] = grad_in[row].astype(F32)
        return mac(
            accs,
            ti,
            6,
            wide,
            lambda i, t: t * ti + i,
            left,
            lambda t: row * cells + t * tj,
            tj,
        )

    def from_gate():
        for h in range(2):

            @pl.when((c == last) & (middle(h) != c))
            def _():
                give_back(h).wait_recv()

            out_linear = dot(norm_back[h], op_ref[...])
            split_a[h] = split_a[h] * out_linear * (1.0 - split_b[h])

        for h in range(2):
            for i in range(ti):
                flat[i * tj + h * ti : i * tj + (h + 1) * ti, :] = split_a[
                    h, i * ti : (i + 1) * ti, :
                ]
        grad_gate[...] = flat[...].astype(BF16)
        total[...] = dot_t(grad_gate[...], og_ref[...])

    def some_grads(first_row, last_row):
        accs = tuple(grad_r[i * tj : (i + 1) * tj, :] for i in range(ti))
        accs = lax.fori_loop(first_row, last_row, take_grad, accs)
        for i, acc in enumerate(accs):
            grad_r[i * tj : (i + 1) * tj, :] = acc

    def from_left():
        back = gate_back(grad_l[...], lin_a[...], sig_a[...])
        return dot_t(jnp.concatenate(back, axis=1), w_left)

    def from_right():
        back = gate_back(grad_r[...], lin_b[...], sig_b[...])
        return dot_t(jnp.concatenate(back, axis=1), w_right)

    lax.fori_loop(0, 2 * cols - 2, forward_take, 0)

    inner = jnp.abs(2 * q - (chips - 1)) * 2 < chips
    soon = jnp.where(inner, 2, 2 * chips - 2)
    grad_r[...] = jnp.zeros((cells, hidden), F32)

    @pl.when(c == q)
    def _():
        from_gate()
        some_grads(0, soon)

    lax.fori_loop(2 * cols - 2, 2 * cols, forward_take, 0)

    @pl.when(c != q)
    def _():
        from_gate()
        total[...] += from_left()
        some_grads(0, rows)
        out_ref[...] = (total[...] + from_right()).astype(BF16)

    @pl.when(c == q)
    def _():
        total[...] += from_left()
        some_grads(soon, rows)
        out_ref[...] = (total[...] + from_right()).astype(BF16)

    def end_chip(d, _):
        first(d, r).wait_send()
        to_sibling(x_ref, r, f_send.at[d]).wait_send()
        return 0

    lax.fori_loop(1, chips, end_chip, 0)
    to_sibling(x_ref, r, a_send.at[0]).wait_send()

    def end_col(d, _):
        col = col_at(d)
        for h in range(2):

            @pl.when(col != last)
            def _():
                part(h, col, c).wait_send()

            @pl.when((c != last) & ((c != q) | jnp.logical_not(beyond(c, col))))
            def _():
                across(h, col, c).wait_send()

            @pl.when((c == gate(q)) & beyond(q, col))
            def _():
                passed(h, col).wait_send()

        @pl.when(central)
        def _():
            across_x(col, side, last).wait_send()

        return 0

    for h in range(2):

        @pl.when(middle(h) != c)
        def _():
            part_x(h, c).wait_send()

            @pl.when(c == last)
            def _():
                lend(h).wait_send()

    @pl.when(central & (c != last))
    def _():
        give_back(side).wait_send()

    lax.fori_loop(1, cols, end_col, 0)

    def end_row(d, _):
        to = row_at(d)
        send(
            panel.at[c, 0], grad_in.at[r], d_send.at[to], d_recv.at[r], to, c
        ).wait_send()
        return 0

    lax.fori_loop(1, rows, end_row, 0)


def body(rows, cols, normed, lp, lg, rp, rg, og, op, gain, keep_bits, cotangent):
    ti, tj, width = normed.shape
    hidden = lp.shape[1]
    assert tj == 2 * ti and rows == 2 * cols
    cells = ti * tj
    half = ti * ti
    tile = pltpu.VMEM((cells, hidden), F32)
    dma = pltpu.SemaphoreType.DMA
    out = pl.pallas_call(
        functools.partial(kernel, rows, cols, ti, tj),
        out_shape=pltpu.VMEM((cells, width), BF16),
        in_specs=[pl.BlockSpec(memory_space=pl.ANY)] * 10,
        out_specs=pl.BlockSpec(memory_space=pltpu.VMEM),
        scratch_shapes=[
            *[pltpu.VMEM((width, hidden), BF16)] * 6,
            pltpu.VMEM((1, hidden), F32),
            pltpu.VMEM(keep_bits.shape[::-1], jnp.int32),
            pltpu.VMEM((cells, width), BF16),
            pltpu.VMEM((cells, width), BF16),
            pltpu.VMEM((rows, cells, width), BF16),
            pltpu.VMEM((rows * cells, hidden), F32),
            pltpu.VMEM((rows * cells, hidden), F32),
            pltpu.VMEM((tj * (-(-ti // 8) * 8), hidden), F32),
            pltpu.VMEM((2, cols, half, hidden), BF16),
            pltpu.VMEM((2, cols, half, hidden), BF16),
            pltpu.VMEM((2, half, hidden), F32),
            tile,
            pltpu.VMEM((2, half, hidden), F32),
            pltpu.VMEM((2, half, hidden), F32),
            pltpu.VMEM((cols, 2, half, hidden), BF16),
            pltpu.VMEM((rows, half, hidden), BF16),
            tile,
            tile,
            tile,
            tile,
            tile,
            tile,
            pltpu.VMEM((cells, width), BF16),
            dma((rows // 2,)),
            dma((rows // 2,)),
            dma((rows,)),
            dma((2, cols)),
            dma((2, cols)),
            dma((2, cols)),
            dma((2, cols)),
            dma((rows,)),
            dma((rows,)),
            dma((10,)),
            tile,
            tile,
            pltpu.VMEM((2, half, hidden), BF16),
            pltpu.VMEM((half, hidden), F32),
            pltpu.VMEM((cols, half, hidden), BF16),
            pltpu.VMEM((half, hidden), BF16),
            pltpu.VMEM((half, hidden), BF16),
            pltpu.VMEM((2, half, hidden), BF16),
            dma((cols,)),
            dma((2,)),
            dma,
            dma((cols,)),
            dma,
            dma((2,)),
            dma((2, cols)),
        ],
        compiler_params=pltpu.CompilerParams(
            collective_id=0, has_side_effects=True, vmem_limit_bytes=56 * 1024 * 1024
        ),
    )(
        normed.reshape(cells, width),
        lp,
        lg,
        rp,
        rg,
        og,
        op,
        gain.reshape(1, hidden),
        keep_bits.T,
        cotangent.reshape(cells, width),
    )
    return out.reshape(ti, tj, width)


def solution(mesh):
    whole = P("row", "col", None)
    return jax.shard_map(
        functools.partial(body, mesh.shape["row"], mesh.shape["col"]),
        mesh=mesh,
        in_specs=(whole, P(), P(), P(), P(), P(), P(), P(), P("col", None), whole),
        out_specs=whole,
        check_vma=False,
    )
```
